256 devices in a mesh: dp: 8 (over z_hi, x), expert: 32 (over z_lo, y, core).
Axes of the slice: x: 4, y: 4, z: 8 (z_hi: 2, z_lo: 4; z = z_hi * 4 + z_lo), core: 2. Of those that a mesh axis runs over, the one named last changes fastest.
Arguments:
- tokens: bfloat16 [8192, 7168], P('expert', 'dp'), may hold values from -6 to 6
- cotangent: bfloat16 [8192, 7168], P('expert', 'dp'), may hold values from -6 to 6
- routing: int32 [8192, 8], P('expert'), may hold values from 0 to 255, as said below
- gate_values: float32 [8192, 8], P('expert'), may hold values from 0.05 to 0.6
- hidden_weight: bfloat16 [32, 7168, 2048], P('expert', 'dp'), may hold values from -0.0625 to 0.0625
- output_weight: bfloat16 [32, 1024, 7168], P('expert', None, 'dp'), may hold values from -0.1875 to 0.1875
Outputs:
- mixed: bfloat16 [8192, 7168], P('expert', 'dp')
- token_grad: bfloat16 [8192, 7168], P('expert', 'dp')
- hidden_grad: bfloat16 [32, 7168, 2048], P('expert', 'dp')
- output_grad: bfloat16 [32, 1024, 7168], P('expert', None, 'dp')
The draws below stay inside these ranges and needn't reach their ends.
Inputs may be any that keep to these rules, and one draw needn't show every extreme that they name: `routing`: each row names 8 different experts. Within the 256 rows of one index of expert no expert is named by more than 16 rows, and in every such block some experts below 32 are named by exactly 16 rows.
All inputs are finite; a program needn't handle non-finite values.
Results may differ from the reference program's by a relative error of at most 0.022.
Values may be sent and summed in bfloat16 or wider, within the bound.
A program may use at most 64 MiB of HBM per device.

```python
import jax
import jax.numpy as jnp
from jax import lax

D = 7168
FFW = 1024
TOP = 8
ROUTED = 256
TOK_DEV = 256
EXPERTS = 32
SLOTS = 16
TOKENS = 8192
N_DP = 8


def draw_routing(key, part):
    blocks = TOKENS // TOK_DEV
    half_count = ROUTED // 2
    ranked_ids = jax.random.permutation(jax.random.fold_in(key, 11), EXPERTS)
    hot_mask = jnp.any(jnp.arange(EXPERTS, dtype=jnp.int32)[:, None] == ranked_ids[None, :3], axis=1)
    levels = jax.random.randint(jax.random.fold_in(key, 12), (blocks, half_count), 0, SLOTS)
    window_level = jax.random.randint(jax.random.fold_in(key, 13), (blocks, EXPERTS), 0, SLOTS)
    window_level = jnp.where(hot_mask[None, :], SLOTS, window_level)
    first_count = jnp.concatenate([window_level, levels[:, EXPERTS:]], axis=1)
    counts = jnp.concatenate([first_count, SLOTS - first_count], axis=1)
    expert_ids = jnp.arange(ROUTED, dtype=jnp.int32)

    def fill_block(count_row, block_key):
        pick_list = jnp.repeat(expert_ids, count_row, total_repeat_length=TOK_DEV * TOP)
        pick_table = pick_list.reshape(TOP, TOK_DEV).T
        shuffled = jax.random.permutation(block_key, TOK_DEV)
        return pick_table[shuffled]
    block_keys = jax.random.split(jax.random.fold_in(key, 14), blocks)
    return jax.vmap(fill_block)(counts, block_keys).reshape(TOKENS, TOP).astype(jnp.int32)


def level_of(key, shape, cuts, low, high):
    gain, own = 1.0, jax.random.fold_in(key, 6)
    for axis_at, parts in cuts:
        steps = jnp.exp(jax.random.uniform(jax.random.fold_in(own, axis_at), (parts,), jnp.float32, low / len(cuts), high / len(cuts)))
        gain = gain * jnp.repeat(steps, shape[axis_at] // parts).reshape([-1 if axis == axis_at else 1 for axis in range(len(shape))])
    return gain


def bell_draw(own_key, dims, deviation, reach, cuts=(), kind=jnp.bfloat16):
    gain = level_of(own_key, dims, cuts, -0.22, 0.18) if cuts else 1.0
    drawn = jax.random.normal(own_key, dims, jnp.float32) * deviation * gain
    return jnp.minimum(jnp.maximum(drawn, -reach), reach).astype(kind)


def setup_inputs(seed: int = 0) -> dict:
    keys = jax.random.split(jax.random.key(seed), 7)
    tokens = bell_draw(keys[0], (TOKENS, D), 1.0, 6.0, ((0, 32), (1, 8)))
    cotangent = bell_draw(keys[1], (TOKENS, D), 1.0, 6.0, ((0, 32), (1, 8)))
    routing = draw_routing(jax.random.fold_in(keys[6], 71), 0)
    gate_values = jnp.clip(0.05 + 0.55 * jax.random.uniform(keys[3], (TOKENS, TOP), jnp.float32) ** level_of(keys[3], (TOKENS, TOP), ((0, 32),), -0.2, 0.2), 0.05, 0.6)
    hidden_weight = bell_draw(keys[4], (EXPERTS, D, 2 * FFW), D ** -0.5, 0.0625, ((0, 32), (1, 8)))
    output_weight = bell_draw(keys[5], (EXPERTS, FFW, D), FFW ** -0.5, 0.1875, ((0, 32), (2, 8)))
    return {"tokens": tokens, "cotangent": cotangent, "routing": routing, "gate_values": gate_values, "hidden_weight": hidden_weight, "output_weight": output_weight}


def slot_table(routing_block, gate_block, expert_count, slot_count):
    tok_count = routing_block.shape[0]
    picked = routing_block.reshape(-1)
    onehot = (picked[:, None] == jnp.arange(expert_count, dtype=jnp.int32)[None, :]).astype(jnp.int32)
    earlier = jnp.cumsum(onehot, axis=0) - onehot
    ranking = lax.optimization_barrier(jnp.sum(earlier * onehot, axis=1))
    slot_index = (picked * slot_count + ranking).reshape(tok_count, -1)
    target = jnp.arange(expert_count * slot_count, dtype=jnp.int32)
    matched = slot_index[None, :, :] == target[:, None, None]
    placed = jnp.any(matched, axis=2).astype(jnp.float32)
    gate_slot = lax.optimization_barrier(jnp.sum(jnp.where(matched, gate_block[None, :, :], jnp.zeros_like(gate_block)[None, :, :]), axis=(1, 2)))
    return (placed, gate_slot)

def activate(hidden, half_width):
    gate_part = hidden[:, :half_width]
    up_part = hidden[:, half_width:]
    return (gate_part * jax.nn.sigmoid(gate_part) * up_part).astype(jnp.bfloat16)

def activate_grad(hidden, act_grad, half_width):
    gate_part = hidden[:, :half_width]
    up_part = hidden[:, half_width:]
    sigmoid_gate = jax.nn.sigmoid(gate_part)
    gate_grad = act_grad * up_part * sigmoid_gate * (1.0 + gate_part * (1.0 - sigmoid_gate))
    up_grad = act_grad * gate_part * sigmoid_gate
    return jnp.concatenate([gate_grad, up_grad], axis=1).astype(jnp.bfloat16)

def blockwise(left_side, right_side, block_count):
    row_count, inner_width = left_side.shape
    block_width = inner_width // block_count
    left_blocks = left_side.astype(jnp.float32).reshape(row_count, block_count, block_width)
    right_blocks = right_side.astype(jnp.float32).reshape(block_count, block_width, right_side.shape[1])
    partial_value = jnp.einsum('rnk,nkf->nrf', left_blocks, right_blocks, precision=lax.Precision.HIGHEST)
    rounded = lax.optimization_barrier(partial_value.astype(jnp.bfloat16))
    return lax.optimization_barrier(jnp.sum(rounded.astype(jnp.float32), axis=0))

def expert_pass(packed):
    rows_in, cot_in, inner_weight, outer_weight = packed
    half_width = outer_weight.shape[0]
    contract_cols = (((1,), (1,)), ((), ()))
    contract_rows = (((0,), (0,)), ((), ()))
    hidden = blockwise(rows_in, inner_weight, N_DP)
    active = activate(hidden, half_width)
    expert_out = jnp.dot(active, outer_weight, preferred_element_type=jnp.float32).astype(jnp.bfloat16)
    act_grad = blockwise(cot_in, outer_weight.T, N_DP)
    hidden_cot = activate_grad(hidden, act_grad, half_width)
    output_grad = lax.dot_general(active, cot_in, contract_rows, preferred_element_type=jnp.float32).astype(jnp.bfloat16)
    hidden_grad = lax.dot_general(rows_in, hidden_cot, contract_rows, preferred_element_type=jnp.float32).astype(jnp.bfloat16)
    row_grad = lax.dot_general(hidden_cot, inner_weight, contract_cols, preferred_element_type=jnp.float32).astype(jnp.bfloat16)
    return (expert_out, row_grad, hidden_grad, output_grad)

def reference(tokens, cotangent, routing, gate_values, hidden_weight, output_weight):
    blocks = TOKENS // TOK_DEV
    highest = lax.Precision.HIGHEST
    tables = jax.vmap(lambda route_block, gate_block: slot_table(route_block, gate_block, EXPERTS, SLOTS))
    placed, gate_slot = tables(routing.reshape(blocks, TOK_DEV, TOP), gate_values.reshape(blocks, TOK_DEV, TOP))
    tok_blocks = tokens.reshape(blocks, TOK_DEV, D).astype(jnp.float32)
    cot_blocks = cotangent.reshape(blocks, TOK_DEV, D).astype(jnp.float32)
    token_rows = jnp.einsum('bst,btd->bsd', placed, tok_blocks, precision=highest).astype(jnp.bfloat16)
    scaled = (gate_slot[:, :, None] * jnp.einsum('bst,btd->bsd', placed, cot_blocks, precision=highest)).astype(jnp.bfloat16)

    def per_expert(values):
        return values.reshape(blocks, EXPERTS, SLOTS, D).transpose(1, 0, 2, 3).reshape(EXPERTS, blocks * SLOTS, D)

    def per_block(values):
        return values.reshape(EXPERTS, blocks, SLOTS, D).transpose(1, 0, 2, 3).reshape(blocks, EXPERTS * SLOTS, D)
    expert_out, row_grad, hidden_grad, output_grad = lax.map(expert_pass, (per_expert(token_rows), per_expert(scaled), hidden_weight, output_weight))
    weighted = placed * gate_slot[:, :, None]
    mixed = jnp.einsum('bst,bsd->btd', weighted, per_block(expert_out).astype(jnp.float32), precision=highest)
    token_grad = jnp.einsum('bst,bsd->btd', placed, per_block(row_grad).astype(jnp.float32), precision=highest)
    mixed = mixed.astype(jnp.bfloat16).reshape(TOKENS, D)
    token_grad = token_grad.astype(jnp.bfloat16).reshape(TOKENS, D)
    return (mixed, token_grad, hidden_grad, output_grad)
```

```python
import functools

import jax
import jax.numpy as jnp
from jax import lax
from jax.experimental import pallas as pl
from jax.experimental.pallas import tpu as pltpu
from jax.sharding import PartitionSpec as P

MESH = pl.DeviceIdType.MESH
F32 = jnp.float32
BF16 = jnp.bfloat16
SLOTS = 16
EXPERTS = 32
CHUNKS = 8
PER = EXPERTS // CHUNKS
SPLIT = CHUNKS // 4
ROWS = PER * SLOTS
NX = 4
QUART = ROWS // NX
VMEM_LIMIT = 40 * 2**20
LAST = (((1,), (1,)), ((), ()))
FIRST = (((0,), (0,)), ((), ()))

SCHEDULE = ('D0', 'D1', 'D2', 'd0', 'D3', 'p0', 't0', 'd1', 'D4', 'p1', 'r0', 'd2', 'D5', 'p2', 'r1', 'z0', 'd3', 'D6', 'p3', 'r2', 'z1', 'g0', 'd4', 'D7', 'p4', 'r3', 'z2', 'g1', 'd5', 'p5', 'r4', 'z3', 'g2', 'd6', 'p6', 'r5', 'z4', 'g3', 'd7', 'p7', 'r6', 'z5', 'g4', 'r7', 'z6', 'g5', 'z7', 'g6', 'g7', 'o0', 'h0', 'c0', 'c1', 'c2', 'c3', 'c4', 'c5', 'c6', 'c7')


def kernel(
    routing_hbm,
    gate_hbm,
    tok_hbm,
    cot_hbm,
    w1_hbm,
    w2_hbm,
    mixed_ref,
    tgrad_ref,
    hgrad_ref,
    ograd_ref,
    routing_ref,
    gate_ref,
    tok_ref,
    cot_ref,
    w1,
    w2,
    place,
    whi,
    wlo,
    send,
    recv,
    part,
    xrecv,
    zsend,
    zrecv,
    act,
    rsend,
    rrecv,
    rows_t,
    place_t,
    whi_t,
    wlo_t,
    mixed_sum,
    grad_sum,
    w_sem,
    d_send,
    d_recv,
    x_send,
    x_recv,
    z_send,
    z_recv,
    g_send,
    g_recv,
    r_send,
    r_recv,
):
    pairs = (
        (routing_hbm, routing_ref),
        (gate_hbm, gate_ref),
        (tok_hbm, tok_ref),
        (cot_hbm, cot_ref),
        (w1_hbm, w1),
        (w2_hbm, w2),
    )
    loads = [pltpu.make_async_copy(*pair, w_sem.at[i]) for i, pair in enumerate(pairs)]
    load1, load2 = loads[4:]
    for load in loads[:4]:
        load.start()
    dp = lax.axis_index("dp")
    me = lax.axis_index("expert")
    zh, x = dp // NX, dp % NX
    zl, y, core = me // 8, (me // 2) % 4, me % 2
    half = w2.shape[0]
    toks = tok_ref.shape[0]
    width = tok_ref.shape[1]
    z_peer = (1 - zh) * NX + x

    def x_peer(i):
        return zh * NX + (x + i) % NX

    def target(c, k):
        if SPLIT == 2:
            return k * 8 + ((y + 4 - c // 2) % 4) * 2 + (core + c) % 2
        return (k // 2) * 8 + ((y + 4 - c) % 4) * 2 + k % 2

    def origin(c, k):
        if SPLIT == 2:
            return k * 8 + ((y + c // 2) % 4) * 2 + (core + c) % 2
        return (k // 2) * 8 + ((y + c) % 4) * 2 + k % 2

    mine = zl if SPLIT == 2 else zl * 2 + core

    barrier = pltpu.get_barrier_semaphore()

    def greet(j, carry):
        pl.semaphore_signal(
            barrier, inc=1, device_id=(dp, (me + j) % EXPERTS), device_id_type=MESH
        )
        return carry

    lax.fori_loop(1, EXPERTS, greet, 0)
    for i in range(1, NX):
        pl.semaphore_signal(barrier, inc=1, device_id=(x_peer(i), me), device_id_type=MESH)
    pl.semaphore_signal(barrier, inc=1, device_id=(z_peer, me), device_id_type=MESH)

    load1.start()
    load2.start()
    loads[0].wait()
    loads[1].wait()

    ids = lax.broadcasted_iota(jnp.int32, (EXPERTS, toks), 0)
    member = jnp.zeros((EXPERTS, toks), F32)
    gates = jnp.zeros((EXPERTS, toks), F32)
    for k in range(routing_ref.shape[0]):
        hit = routing_ref[k : k + 1, :] == ids
        member = jnp.where(hit, 1.0, member)
        gates = jnp.where(hit, gate_ref[k : k + 1, :], gates)
    earlier = lax.broadcasted_iota(jnp.int32, (toks, toks), 0) < lax.broadcasted_iota(
        jnp.int32, (toks, toks), 1
    )
    earlier = jnp.where(earlier, 1.0, 0.0).astype(BF16)
    rank = jnp.dot(member.astype(BF16), earlier, preferred_element_type=F32)
    rank = jnp.where(member > 0.0, rank, -1.0).astype(BF16)
    slots = EXPERTS * SLOTS
    order = lax.broadcasted_iota(jnp.int32, (slots, EXPERTS), 0) >> 4
    spread = target(order // PER, order % PER) == lax.broadcasted_iota(
        jnp.int32, (slots, EXPERTS), 1
    )
    spread = jnp.where(spread, 1.0, 0.0).astype(BF16)
    within = lax.broadcasted_iota(jnp.int32, (slots, toks), 0) & (SLOTS - 1)
    hits = jnp.dot(spread, rank, preferred_element_type=F32) == within.astype(F32)
    high = gates.astype(BF16)
    low = (gates - high.astype(F32)).astype(BF16)
    place[...] = jnp.where(hits, 1.0, 0.0).astype(BF16)
    whi[...] = jnp.where(
        hits, jnp.dot(spread, high, preferred_element_type=F32), 0.0
    ).astype(BF16)
    wlo[...] = jnp.where(
        hits, jnp.dot(spread, low, preferred_element_type=F32), 0.0
    ).astype(BF16)

    def pick(c):
        at = pl.ds(c * ROWS, ROWS)
        rows = jnp.dot(place[at, :], tok_ref[...], preferred_element_type=F32)
        send[c, :, 0] = rows.astype(BF16).reshape(PER, SLOTS, width)
        rows = jnp.dot(whi[at, :], cot_ref[...], preferred_element_type=F32)
        rows += jnp.dot(wlo[at, :], cot_ref[...], preferred_element_type=F32)
        send[c, :, 1] = rows.astype(BF16).reshape(PER, SLOTS, width)

    def dispatch_copy(c, j):
        k = (mine + j) % PER
        to = target(c, k)
        return pltpu.make_async_remote_copy(
            src_ref=send.at[c, k],
            dst_ref=recv.at[c, mine],
            send_sem=d_send.at[c, j],
            recv_sem=d_recv.at[c, mine],
            device_id=(dp, to),
            device_id_type=MESH,
        )

    def own_dispatch():
        return pltpu.make_async_copy(
            send.at[0, mine], recv.at[0, mine], d_recv.at[0, mine]
        )

    def return_copy(c, j):
        k = (mine + j) % PER
        to = origin(c, k)
        return pltpu.make_async_remote_copy(
            src_ref=rsend.at[c, k],
            dst_ref=rrecv.at[c, mine],
            send_sem=r_send.at[c, j],
            recv_sem=r_recv.at[c, mine],
            device_id=(dp, to),
            device_id_type=MESH,
        )

    def own_return():
        return pltpu.make_async_copy(
            rsend.at[0, mine], rrecv.at[0, mine], r_recv.at[0, mine]
        )

    def scatter_copy(c, i):
        to = (x + i) % NX
        return pltpu.make_async_remote_copy(
            src_ref=part.at[c, pl.ds(to * QUART, QUART)],
            dst_ref=xrecv.at[c, i - 1],
            send_sem=x_send.at[c, i - 1],
            recv_sem=x_recv.at[c, i - 1],
            device_id=(x_peer(i), me),
            device_id_type=MESH,
        )

    def exchange_copy(c):
        return pltpu.make_async_remote_copy(
            src_ref=zsend.at[c],
            dst_ref=zrecv.at[c],
            send_sem=z_send.at[c],
            recv_sem=z_recv.at[c],
            device_id=(z_peer, me),
            device_id_type=MESH,
        )

    def gather_copy(c, i, owner):
        block = pl.ds(owner * QUART, QUART)
        return pltpu.make_async_remote_copy(
            src_ref=act.at[c, block],
            dst_ref=act.at[c, block],
            send_sem=g_send.at[c, i - 1],
            recv_sem=g_recv.at[c, i - 1],
            device_id=(x_peer(i), me),
            device_id_type=MESH,
        )

    def start_dispatch(c):
        if c > 0:
            pick(c)
        else:
            own_dispatch().start()

        def one(j, carry):
            dispatch_copy(c, j).start()
            return carry

        lax.fori_loop(1 if c == 0 else 0, PER, one, 0)

    def wait_dispatch(c):
        def one(k, carry):
            pltpu.make_async_copy(recv.at[c, k], recv.at[c, k], d_recv.at[c, k]).wait()
            return carry

        lax.fori_loop(0, PER, one, 0)

    def products(c):
        if c == 0:
            load1.wait()
            load2.wait()
        tok_rows = recv[c, :, 0].reshape(ROWS, width)
        cot_rows = recv[c, :, 1].reshape(ROWS, width)
        tile = 512

        def hidden_tile(n, carry):
            at = pl.ds(pl.multiple_of(n * tile, tile), tile)
            part[c, :, at] = jnp.dot(
                recv[c, :, 0].reshape(ROWS, width), w1[:, at], preferred_element_type=F32
            ).astype(BF16)
            return carry

        lax.fori_loop(0, 2 * half // tile, hidden_tile, 0)

        def act_tile(n, carry):
            at = pl.ds(pl.multiple_of(n * tile, tile), tile)
            to = pl.ds(pl.multiple_of(2 * half + n * tile, tile), tile)
            part[c, :, to] = lax.dot_general(
                recv[c, :, 1].reshape(ROWS, width), w2[at, :], LAST, preferred_element_type=F32
            ).astype(BF16)
            return carry

        lax.fori_loop(0, half // tile, act_tile, 0)
        for i in range(1, NX):
            scatter_copy(c, i).start()

    def reduce_x(c):
        for i in range(1, NX):
            scatter_copy(c, i).wait_recv()
        own = part[c, pl.ds(pl.multiple_of(x * QUART, QUART), QUART)].astype(F32)
        total = own + xrecv[c, 0].astype(F32)
        total += xrecv[c, 1].astype(F32)
        total += xrecv[c, 2].astype(F32)
        zsend[c] = total.astype(BF16)
        exchange_copy(c).start()

    def activate(c):
        exchange_copy(c).wait_recv()
        total = zsend[c].astype(F32) + zrecv[c].astype(F32)
        gate = total[:, :half]
        up = total[:, half : 2 * half]
        grad = total[:, 2 * half :]
        sig = jax.nn.sigmoid(gate)
        silu = gate * sig
        block = pl.ds(pl.multiple_of(x * QUART, QUART), QUART)
        act[c, block, 0:half] = (silu * up).astype(BF16)
        act[c, block, half : 2 * half] = (
            grad * up * sig * (1.0 + gate * (1.0 - sig))
        ).astype(BF16)
        act[c, block, 2 * half :] = (grad * silu).astype(BF16)
        for i in range(1, NX):
            gather_copy(c, i, x).start()

    def results(c):
        for i in range(1, NX):
            gather_copy(c, i, (x + NX - i) % NX).wait_recv()
        out = jnp.dot(act[c, :, 0:half], w2[...], preferred_element_type=F32)
        rsend[c, :, 0] = out.astype(BF16).reshape(PER, SLOTS, width)
        out = lax.dot_general(
            act[c, :, half:], w1[...], LAST, preferred_element_type=F32
        )
        rsend[c, :, 1] = out.astype(BF16).reshape(PER, SLOTS, width)
        if c == 0:
            own_return().start()

        def one(j, carry):
            return_copy(c, j).start()
            return carry

        lax.fori_loop(1 if c == 0 else 0, PER, one, 0)

    def transposes():
        place_t[...] = place[...].T
        whi_t[...] = whi[...].T
        wlo_t[...] = wlo[...].T

    def combine(c):
        def arrived(k, carry):
            pltpu.make_async_copy(rrecv.at[c, k], rrecv.at[c, k], r_recv.at[c, k]).wait()
            return carry

        lax.fori_loop(0, PER, arrived, 0)
        at = pl.ds(c * ROWS, ROWS)
        back = rrecv[c, :, 0].reshape(ROWS, width)
        mixed = jnp.dot(whi_t[:, at], back, preferred_element_type=F32)
        mixed += jnp.dot(wlo_t[:, at], back, preferred_element_type=F32)
        back = rrecv[c, :, 1].reshape(ROWS, width)
        grads = jnp.dot(place_t[:, at], back, preferred_element_type=F32)
        if c > 0:
            mixed += mixed_sum[...]
            grads += grad_sum[...]
        if c < CHUNKS - 1:
            mixed_sum[...] = mixed
            grad_sum[...] = grads
        else:
            mixed_ref[...] = mixed.astype(BF16)
            tgrad_ref[...] = grads.astype(BF16)

    loads[2].wait()
    loads[3].wait()
    pick(0)
    pl.semaphore_wait(barrier, EXPERTS - 1 + NX)

    run = {
        "D": start_dispatch,
        "d": wait_dispatch,
        "p": products,
        "r": reduce_x,
        "z": activate,
        "g": results,
    }
    def output_gradient(_):
        tile = 256

        def one(n, carry):
            at = pl.ds(pl.multiple_of(n * tile, tile), tile)
            ograd_ref[at, :] = lax.dot_general(
                act[:, :, at].reshape(slots, tile),
                recv[:, :, 1].reshape(slots, width),
                FIRST,
                preferred_element_type=F32,
            ).astype(BF16)
            return carry

        lax.fori_loop(0, half // tile, one, 0)

    def hidden_gradient(_):
        tile = 256
        rows_t[...] = recv[:, :, 0].reshape(slots, width).T

        def one(n, carry):
            at = pl.ds(pl.multiple_of(n * tile, tile), tile)
            cots = act[:, :, pl.ds(pl.multiple_of(half + n * tile, tile), tile)]
            hgrad_ref[:, at] = jnp.dot(
                rows_t[...], cots.reshape(slots, tile), preferred_element_type=F32
            ).astype(BF16)
            return carry

        lax.fori_loop(0, 2 * half // tile, one, 0)

    run["t"] = lambda _: transposes()
    run["o"] = output_gradient
    run["h"] = hidden_gradient
    run["c"] = combine
    for step in SCHEDULE:
        run[step[0]](int(step[1]))

    for c in range(CHUNKS):

        def left(j, carry):
            dispatch_copy(c, j).wait_send()
            return_copy(c, j).wait_send()
            return carry

        lax.fori_loop(1 if c == 0 else 0, PER, left, 0)
        for i in range(1, NX):
            scatter_copy(c, i).wait_send()
            gather_copy(c, i, x).wait_send()
        exchange_copy(c).wait_send()


def store_kernel(*refs):
    ins, outs, sem = refs[:4], refs[4:8], refs[8]
    copies = [
        pltpu.make_async_copy(ins[i], outs[i], sem.at[i]) for i in range(4)
    ]
    for copy in copies:
        copy.start()
    for copy in copies:
        copy.wait()


def body(tokens, cotangent, routing, gate_values, hidden_weight, output_weight):
    toks, width = tokens.shape
    half = output_weight.shape[1]
    wide = 3 * half
    dma = pltpu.SemaphoreType.DMA
    vmem = pl.BlockSpec(memory_space=pltpu.VMEM)
    hbm = pl.BlockSpec(memory_space=pltpu.HBM)
    shapes = ((toks, width), (toks, width), (width, 2 * half), (half, width))
    slots = EXPERTS * SLOTS
    made = pl.pallas_call(
        kernel,
        name="moe_layer",
        out_shape=[pltpu.VMEM(shape, BF16) for shape in shapes],
        in_specs=[hbm] * 6,
        out_specs=[vmem] * 4,
        scratch_shapes=[
            pltpu.VMEM(routing.shape[::-1], jnp.int32),
            pltpu.VMEM(routing.shape[::-1], F32),
            pltpu.VMEM((toks, width), BF16),
            pltpu.VMEM((toks, width), BF16),
            pltpu.VMEM((width, 2 * half), BF16),
            pltpu.VMEM((half, width), BF16),
            pltpu.VMEM((slots, toks), BF16),
            pltpu.VMEM((slots, toks), BF16),
            pltpu.VMEM((slots, toks), BF16),
            pltpu.VMEM((CHUNKS, PER, 2, SLOTS, width), BF16),
            pltpu.VMEM((CHUNKS, PER, 2, SLOTS, width), BF16),
            pltpu.VMEM((CHUNKS, ROWS, wide), BF16),
            pltpu.VMEM((CHUNKS, NX - 1, QUART, wide), BF16),
            pltpu.VMEM((CHUNKS, QUART, wide), BF16),
            pltpu.VMEM((CHUNKS, QUART, wide), BF16),
            pltpu.VMEM((CHUNKS, ROWS, wide), BF16),
            pltpu.VMEM((CHUNKS, PER, 2, SLOTS, width), BF16),
            pltpu.VMEM((CHUNKS, PER, 2, SLOTS, width), BF16),
            pltpu.VMEM((width, slots), BF16),
            pltpu.VMEM((toks, slots), BF16),
            pltpu.VMEM((toks, slots), BF16),
            pltpu.VMEM((toks, slots), BF16),
            pltpu.VMEM((toks, width), F32),
            pltpu.VMEM((toks, width), F32),
            dma((6,)),
            dma((CHUNKS, PER)),
            dma((CHUNKS, PER)),
            dma((CHUNKS, NX - 1)),
            dma((CHUNKS, NX - 1)),
            dma((CHUNKS,)),
            dma((CHUNKS,)),
            dma((CHUNKS, NX - 1)),
            dma((CHUNKS, NX - 1)),
            dma((CHUNKS, PER)),
            dma((CHUNKS, PER)),
        ],
        compiler_params=pltpu.CompilerParams(
            collective_id=0, has_side_effects=True, vmem_limit_bytes=VMEM_LIMIT
        ),
    )(
        *[
            pltpu.with_memory_space_constraint(value, pltpu.HBM)
            for value in (
                routing.T,
                gate_values.T,
                tokens,
                cotangent,
                hidden_weight[0],
                output_weight[0],
            )
        ]
    )
    made = [pltpu.with_memory_space_constraint(value, pltpu.VMEM) for value in made]
    mixed, token_grad, hidden_grad, output_grad = pl.pallas_call(
        store_kernel,
        name="store",
        out_shape=[jax.ShapeDtypeStruct(shape, BF16) for shape in shapes],
        in_specs=[vmem] * 4,
        out_specs=[hbm] * 4,
        scratch_shapes=[dma((4,))],
        compiler_params=pltpu.CompilerParams(vmem_limit_bytes=2**20),
    )(*made)
    return mixed, token_grad, hidden_grad[None], output_grad[None]


def solution(mesh):
    return jax.shard_map(
        body,
        mesh=mesh,
        in_specs=(
            P("expert", "dp"),
            P("expert", "dp"),
            P("expert", None),
            P("expert", None),
            P("expert", "dp", None),
            P("expert", None, "dp"),
        ),
        out_specs=(
            P("expert", "dp"),
            P("expert", "dp"),
            P("expert", "dp", None),
            P("expert", None, "dp"),
        ),
        check_vma=False,
    )
```

```python
import functools

import jax
import jax.numpy as jnp
from jax import lax
from jax.experimental import pallas as pl
from jax.experimental.pallas import tpu as pltpu
from jax.sharding import PartitionSpec as P

MESH = pl.DeviceIdType.MESH
F32 = jnp.float32
BF16 = jnp.bfloat16
SLOTS = 16
EXPERTS = 32
CHUNKS = 8
PER = EXPERTS // CHUNKS
SPLIT = CHUNKS // 4
ROWS = PER * SLOTS
NX = 4
QUART = ROWS // NX
VMEM_LIMIT = 40 * 2**20
STORES = 4
XP = 1
ZP = 3
AP = 1
DP = 2
RP = 1
LAST = (((1,), (1,)), ((), ()))
FIRST = (((0,), (0,)), ((), ()))

SCHEDULE = ('D0', 'D1', 'D2', 'D3', 'D4', 'D5', 'D6', 'D7', 'd0', 'p0', 't0', 'd1', 'p1', 'r0', 'd2', 'p2', 'r1', 'z0', 'd3', 'p3', 'r2', 'z1', 'g0', 'd4', 'p4', 'r3', 'z2', 'g1', 'd5', 'p5', 'r4', 'z3', 'g2', 'd6', 'p6', 'r5', 'z4', 'g3', 'd7', 'p7', 'r6', 'z5', 'g4', 'r7', 'z6', 'g5', 'z7', 'g6', 'g7', 'o0', 'h0', 'c0', 'c1', 'c2', 'c3', 'c4', 'c5', 'c6', 'c7')


def kernel(
    routing_hbm,
    gate_hbm,
    tok_hbm,
    cot_hbm,
    w1_hbm,
    w2_hbm,
    mixed_ref,
    tgrad_ref,
    hgrad_ref,
    ograd_ref,
    routing_ref,
    gate_ref,
    tok_ref,
    cot_ref,
    w1,
    w2,
    place,
    whi,
    wlo,
    send,
    recv,
    part,
    xrecv,
    zsend,
    zrecv,
    act,
    rsend,
    rrecv,
    rows_t,
    place_t,
    whi_t,
    wlo_t,
    mixed_sum,
    grad_sum,
    w_sem,
    d_send,
    d_recv,
    x_send,
    x_recv,
    z_send,
    z_recv,
    g_send,
    g_recv,
    r_send,
    r_recv,
):
    pairs = (
        (routing_hbm, routing_ref),
        (gate_hbm, gate_ref),
        (tok_hbm, tok_ref),
        (cot_hbm, cot_ref),
        (w1_hbm, w1),
        (w2_hbm, w2),
    )
    loads = [pltpu.make_async_copy(*pair, w_sem.at[i]) for i, pair in enumerate(pairs)]
    load1, load2 = loads[4:]
    for load in loads[:4]:
        load.start()
    dp = lax.axis_index("dp")
    me = lax.axis_index("expert")
    zh, x = dp // NX, dp % NX
    zl, y, core = me // 8, (me // 2) % 4, me % 2
    half = w2.shape[0]
    toks = tok_ref.shape[0]
    width = tok_ref.shape[1]
    z_peer = (1 - zh) * NX + x

    def x_peer(i):
        return zh * NX + (x + i) % NX

    def target(c, k):
        if SPLIT == 2:
            return k * 8 + ((y + 4 - c // 2) % 4) * 2 + (core + c) % 2
        return (k // 2) * 8 + ((y + 4 - c) % 4) * 2 + k % 2

    def origin(c, k):
        if SPLIT == 2:
            return k * 8 + ((y + c // 2) % 4) * 2 + (core + c) % 2
        return (k // 2) * 8 + ((y + c) % 4) * 2 + k % 2

    mine = zl if SPLIT == 2 else zl * 2 + core

    barrier = pltpu.get_barrier_semaphore()

    def greet(j, carry):
        pl.semaphore_signal(
            barrier, inc=1, device_id=(dp, (me + j) % EXPERTS), device_id_type=MESH
        )
        return carry

    lax.fori_loop(1, EXPERTS, greet, 0)
    for i in range(1, NX):
        pl.semaphore_signal(barrier, inc=1, device_id=(x_peer(i), me), device_id_type=MESH)
    pl.semaphore_signal(barrier, inc=1, device_id=(z_peer, me), device_id_type=MESH)

    load1.start()
    load2.start()
    loads[0].wait()
    loads[1].wait()

    ids = lax.broadcasted_iota(jnp.int32, (EXPERTS, toks), 0)
    member = jnp.zeros((EXPERTS, toks), F32)
    gates = jnp.zeros((EXPERTS, toks), F32)
    for k in range(routing_ref.shape[0]):
        hit = routing_ref[k : k + 1, :] == ids
        member = jnp.where(hit, 1.0, member)
        gates = jnp.where(hit, gate_ref[k : k + 1, :], gates)
    earlier = lax.broadcasted_iota(jnp.int32, (toks, toks), 0) < lax.broadcasted_iota(
        jnp.int32, (toks, toks), 1
    )
    earlier = jnp.where(earlier, 1.0, 0.0).astype(BF16)
    rank = jnp.dot(member.astype(BF16), earlier, preferred_element_type=F32)
    rank = jnp.where(member > 0.0, rank, -1.0).astype(BF16)
    slots = EXPERTS * SLOTS
    order = lax.broadcasted_iota(jnp.int32, (slots, EXPERTS), 0) >> 4
    spread = target(order // PER, order % PER) == lax.broadcasted_iota(
        jnp.int32, (slots, EXPERTS), 1
    )
    spread = jnp.where(spread, 1.0, 0.0).astype(BF16)
    within = lax.broadcasted_iota(jnp.int32, (slots, toks), 0) & (SLOTS - 1)
    hits = jnp.dot(spread, rank, preferred_element_type=F32) == within.astype(F32)
    high = gates.astype(BF16)
    low = (gates - high.astype(F32)).astype(BF16)
    place[...] = jnp.where(hits, 1.0, 0.0).astype(BF16)

    def gate_tables():
        whi[...] = jnp.where(
            hits, jnp.dot(spread, high, preferred_element_type=F32), 0.0
        ).astype(BF16)
        wlo[...] = jnp.where(
            hits, jnp.dot(spread, low, preferred_element_type=F32), 0.0
        ).astype(BF16)

    def pick_tokens(c):
        at = pl.ds(c * ROWS, ROWS)
        rows = jnp.dot(place[at, :], tok_ref[...], preferred_element_type=F32)
        send[c, :, 0] = rows.astype(BF16).reshape(PER, SLOTS, width)

    def pick_cotangents(c):
        at = pl.ds(c * ROWS, ROWS)
        rows = jnp.dot(whi[at, :], cot_ref[...], preferred_element_type=F32)
        rows += jnp.dot(wlo[at, :], cot_ref[...], preferred_element_type=F32)
        send[c, :, 1] = rows.astype(BF16).reshape(PER, SLOTS, width)

    def rows_part(ref, q, pieces):
        return ref if pieces == 1 else ref.at[q]

    def columns(q, pieces):
        return pl.ds(q * (3 * half // pieces), 3 * half // pieces)

    def dispatch_copy(c, j, q):
        k = (mine + j) % PER
        to = target(c, k)
        return pltpu.make_async_remote_copy(
            src_ref=rows_part(send.at[c, k], q, DP),
            dst_ref=rows_part(recv.at[c, mine], q, DP),
            send_sem=d_send.at[c, q, j],
            recv_sem=d_recv.at[c, q, mine],
            device_id=(dp, to),
            device_id_type=MESH,
        )

    def own_dispatch(q):
        return pltpu.make_async_copy(
            rows_part(send.at[0, mine], q, DP),
            rows_part(recv.at[0, mine], q, DP),
            d_recv.at[0, q, mine],
        )

    def return_copy(c, j, q):
        k = (mine + j) % PER
        to = origin(c, k)
        return pltpu.make_async_remote_copy(
            src_ref=rows_part(rsend.at[c, k], q, RP),
            dst_ref=rows_part(rrecv.at[c, mine], q, RP),
            send_sem=r_send.at[c, q, j],
            recv_sem=r_recv.at[c, q, mine],
            device_id=(dp, to),
            device_id_type=MESH,
        )

    def own_return(q):
        return pltpu.make_async_copy(
            rows_part(rsend.at[0, mine], q, RP),
            rows_part(rrecv.at[0, mine], q, RP),
            r_recv.at[0, q, mine],
        )

    def scatter_copy(c, i, q):
        to = (x + i) % NX
        return pltpu.make_async_remote_copy(
            src_ref=part.at[c, pl.ds(to * QUART, QUART), columns(q, XP)],
            dst_ref=xrecv.at[c, i - 1, :, columns(q, XP)],
            send_sem=x_send.at[c, i - 1, q],
            recv_sem=x_recv.at[c, i - 1, q],
            device_id=(x_peer(i), me),
            device_id_type=MESH,
        )

    def exchange_copy(c, q):
        return pltpu.make_async_remote_copy(
            src_ref=zsend.at[c, :, columns(q, ZP)],
            dst_ref=zrecv.at[c, :, columns(q, ZP)],
            send_sem=z_send.at[c, q],
            recv_sem=z_recv.at[c, q],
            device_id=(z_peer, me),
            device_id_type=MESH,
        )

    def gather_copy(c, i, owner, q):
        block = pl.ds(owner * QUART, QUART)
        return pltpu.make_async_remote_copy(
            src_ref=act.at[c, block, columns(q, AP)],
            dst_ref=act.at[c, block, columns(q, AP)],
            send_sem=g_send.at[c, i - 1, q],
            recv_sem=g_recv.at[c, i - 1, q],
            device_id=(x_peer(i), me),
            device_id_type=MESH,
        )

    def send_rows(c, q):
        if c == 0:
            own_dispatch(q).start()

        def one(j, carry):
            dispatch_copy(c, j, q).start()
            return carry

        lax.fori_loop(1 if c == 0 else 0, PER, one, 0)

    def start_dispatch(c):
        if c > 0:
            pick_tokens(c)
        if DP == 2:
            send_rows(c, 0)
        if c == 0:
            gate_tables()
            loads[3].wait()
        pick_cotangents(c)
        send_rows(c, DP - 1)

    def wait_rows(c, q):
        def one(k, carry):
            block = rows_part(recv.at[c, k], q, DP)
            pltpu.make_async_copy(block, block, d_recv.at[c, q, k]).wait()
            return carry

        lax.fori_loop(0, PER, one, 0)

    def wait_dispatch(c):
        pass

    def products(c):
        if c == 0:
            load1.wait()
            load2.wait()
        wait_rows(c, 0)
        tile = 512

        def hidden_tile(n, carry):
            at = pl.ds(pl.multiple_of(n * tile, tile), tile)
            part[c, :, at] = jnp.dot(
                recv[c, :, 0].reshape(ROWS, width), w1[:, at], preferred_element_type=F32
            ).astype(BF16)
            return carry

        lax.fori_loop(0, 2 * half // tile, hidden_tile, 0)
        if XP == 3:
            for q in range(2):
                for i in range(1, NX):
                    scatter_copy(c, i, q).start()
        if DP == 2:
            wait_rows(c, 1)

        def act_tile(n, carry):
            at = pl.ds(pl.multiple_of(n * tile, tile), tile)
            to = pl.ds(pl.multiple_of(2 * half + n * tile, tile), tile)
            part[c, :, to] = lax.dot_general(
                recv[c, :, 1].reshape(ROWS, width), w2[at, :], LAST, preferred_element_type=F32
            ).astype(BF16)
            return carry

        lax.fori_loop(0, half // tile, act_tile, 0)
        for q in range(2 if XP == 3 else 0, XP):
            for i in range(1, NX):
                scatter_copy(c, i, q).start()

    def reduce_x(c):
        for q in range(XP):
            for i in range(1, NX):
                scatter_copy(c, i, q).wait_recv()
        own = part[c, pl.ds(pl.multiple_of(x * QUART, QUART), QUART)].astype(F32)
        total = own + xrecv[c, 0].astype(F32)
        total += xrecv[c, 1].astype(F32)
        total += xrecv[c, 2].astype(F32)
        zsend[c] = total.astype(BF16)
        for q in range(ZP):
            exchange_copy(c, q).start()

    def activate(c):
        for q in range(ZP):
            exchange_copy(c, q).wait_recv()
        total = zsend[c].astype(F32) + zrecv[c].astype(F32)
        gate = total[:, :half]
        up = total[:, half : 2 * half]
        grad = total[:, 2 * half :]
        sig = jax.nn.sigmoid(gate)
        silu = gate * sig
        block = pl.ds(pl.multiple_of(x * QUART, QUART), QUART)
        act[c, block, 0:half] = (silu * up).astype(BF16)
        act[c, block, half : 2 * half] = (
            grad * up * sig * (1.0 + gate * (1.0 - sig))
        ).astype(BF16)
        act[c, block, 2 * half :] = (grad * silu).astype(BF16)
        for q in range(AP):
            for i in range(1, NX):
                gather_copy(c, i, x, q).start()

    def results(c):
        for q in range(AP):
            for i in range(1, NX):
                gather_copy(c, i, (x + NX - i) % NX, q).wait_recv()
        out = jnp.dot(act[c, :, 0:half], w2[...], preferred_element_type=F32)
        rsend[c, :, 0] = out.astype(BF16).reshape(PER, SLOTS, width)
        if RP == 2:
            send_results(c, 0)
        out = lax.dot_general(
            act[c, :, half:], w1[...], LAST, preferred_element_type=F32
        )
        rsend[c, :, 1] = out.astype(BF16).reshape(PER, SLOTS, width)
        send_results(c, RP - 1)

    def send_results(c, q):
        if c == 0:
            own_return(q).start()

        def one(j, carry):
            return_copy(c, j, q).start()
            return carry

        lax.fori_loop(1 if c == 0 else 0, PER, one, 0)

    def transposes():
        place_t[...] = place[...].T
        whi_t[...] = whi[...].T
        wlo_t[...] = wlo[...].T

    def combine(c):
        def arrived(k, carry):
            for q in range(RP):
                block = rows_part(rrecv.at[c, k], q, RP)
                pltpu.make_async_copy(block, block, r_recv.at[c, q, k]).wait()
            return carry

        lax.fori_loop(0, PER, arrived, 0)
        at = pl.ds(c * ROWS, ROWS)
        back = rrecv[c, :, 0].reshape(ROWS, width)
        mixed = jnp.dot(whi_t[:, at], back, preferred_element_type=F32)
        mixed += jnp.dot(wlo_t[:, at], back, preferred_element_type=F32)
        back = rrecv[c, :, 1].reshape(ROWS, width)
        grads = jnp.dot(place_t[:, at], back, preferred_element_type=F32)
        if c > 0:
            mixed += mixed_sum[...]
            grads += grad_sum[...]
        if c < CHUNKS - 1:
            mixed_sum[...] = mixed
            grad_sum[...] = grads
        else:
            mixed_ref[...] = mixed.astype(BF16)
            tgrad_ref[...] = grads.astype(BF16)

    loads[2].wait()
    pick_tokens(0)
    pl.semaphore_wait(barrier, EXPERTS - 1 + NX)

    run = {
        "D": start_dispatch,
        "d": wait_dispatch,
        "p": products,
        "r": reduce_x,
        "z": activate,
        "g": results,
    }
    def output_gradient(_):
        tile = 256

        def one(n, carry):
            at = pl.ds(pl.multiple_of(n * tile, tile), tile)
            ograd_ref[at, :] = lax.dot_general(
                act[:, :, at].reshape(slots, tile),
                recv[:, :, 1].reshape(slots, width),
                FIRST,
                preferred_element_type=F32,
            ).astype(BF16)
            return carry

        lax.fori_loop(0, half // tile, one, 0)

    def hidden_gradient(_):
        tile = 256
        rows_t[...] = recv[:, :, 0].reshape(slots, width).T

        def one(n, carry):
            at = pl.ds(pl.multiple_of(n * tile, tile), tile)
            cots = act[:, :, pl.ds(pl.multiple_of(half + n * tile, tile), tile)]
            hgrad_ref[:, at] = jnp.dot(
                rows_t[...], cots.reshape(slots, tile), preferred_element_type=F32
            ).astype(BF16)
            return carry

        lax.fori_loop(0, 2 * half // tile, one, 0)

    run["t"] = lambda _: transposes()
    run["o"] = output_gradient
    run["h"] = hidden_gradient
    run["c"] = combine
    for step in SCHEDULE:
        run[step[0]](int(step[1]))

    for c in range(CHUNKS):

        def left(j, carry):
            for q in range(DP):
                dispatch_copy(c, j, q).wait_send()
            for q in range(RP):
                return_copy(c, j, q).wait_send()
            return carry

        lax.fori_loop(1 if c == 0 else 0, PER, left, 0)
        for i in range(1, NX):
            for q in range(XP):
                scatter_copy(c, i, q).wait_send()
            for q in range(AP):
                gather_copy(c, i, x, q).wait_send()
        for q in range(ZP):
            exchange_copy(c, q).wait_send()


def store_kernel(*refs):
    ins, outs, sem = refs[:4], refs[4:8], refs[8]
    copies = []
    for ref, out in zip(ins, outs):
        parts = STORES if ref.shape[0] > ins[0].shape[0] else 1
        rows = ref.shape[0] // parts
        for n in range(parts):
            at = pl.ds(n * rows, rows)
            copies.append(
                pltpu.make_async_copy(ref.at[at], out.at[at], sem.at[len(copies)])
            )
    for copy in copies:
        copy.start()
    for copy in copies:
        copy.wait()


def body(tokens, cotangent, routing, gate_values, hidden_weight, output_weight):
    toks, width = tokens.shape
    half = output_weight.shape[1]
    wide = 3 * half
    dma = pltpu.SemaphoreType.DMA
    vmem = pl.BlockSpec(memory_space=pltpu.VMEM)
    hbm = pl.BlockSpec(memory_space=pltpu.HBM)
    shapes = ((toks, width), (toks, width), (width, 2 * half), (half, width))
    slots = EXPERTS * SLOTS
    made = pl.pallas_call(
        kernel,
        name="moe_layer",
        out_shape=[pltpu.VMEM(shape, BF16) for shape in shapes],
        in_specs=[hbm] * 6,
        out_specs=[vmem] * 4,
        scratch_shapes=[
            pltpu.VMEM(routing.shape[::-1], jnp.int32),
            pltpu.VMEM(routing.shape[::-1], F32),
            pltpu.VMEM((toks, width), BF16),
            pltpu.VMEM((toks, width), BF16),
            pltpu.VMEM((width, 2 * half), BF16),
            pltpu.VMEM((half, width), BF16),
            pltpu.VMEM((slots, toks), BF16),
            pltpu.VMEM((slots, toks), BF16),
            pltpu.VMEM((slots, toks), BF16),
            pltpu.VMEM((CHUNKS, PER, 2, SLOTS, width), BF16),
            pltpu.VMEM((CHUNKS, PER, 2, SLOTS, width), BF16),
            pltpu.VMEM((CHUNKS, ROWS, wide), BF16),
            pltpu.VMEM((CHUNKS, NX - 1, QUART, wide), BF16),
            pltpu.VMEM((CHUNKS, QUART, wide), BF16),
            pltpu.VMEM((CHUNKS, QUART, wide), BF16),
            pltpu.VMEM((CHUNKS, ROWS, wide), BF16),
            pltpu.VMEM((CHUNKS, PER, 2, SLOTS, width), BF16),
            pltpu.VMEM((CHUNKS, PER, 2, SLOTS, width), BF16),
            pltpu.VMEM((width, slots), BF16),
            pltpu.VMEM((toks, slots), BF16),
            pltpu.VMEM((toks, slots), BF16),
            pltpu.VMEM((toks, slots), BF16),
            pltpu.VMEM((toks, width), F32),
            pltpu.VMEM((toks, width), F32),
            dma((6,)),
            dma((CHUNKS, DP, PER)),
            dma((CHUNKS, DP, PER)),
            dma((CHUNKS, NX - 1, XP)),
            dma((CHUNKS, NX - 1, XP)),
            dma((CHUNKS, ZP)),
            dma((CHUNKS, ZP)),
            dma((CHUNKS, NX - 1, AP)),
            dma((CHUNKS, NX - 1, AP)),
            dma((CHUNKS, RP, PER)),
            dma((CHUNKS, RP, PER)),
        ],
        compiler_params=pltpu.CompilerParams(
            collective_id=0, has_side_effects=True, vmem_limit_bytes=VMEM_LIMIT
        ),
    )(
        *[
            pltpu.with_memory_space_constraint(value, pltpu.HBM)
            for value in (
                routing.T,
                gate_values.T,
                tokens,
                cotangent,
                hidden_weight[0],
                output_weight[0],
            )
        ]
    )
    made = [pltpu.with_memory_space_constraint(value, pltpu.VMEM) for value in made]
    mixed, token_grad, hidden_grad, output_grad = pl.pallas_call(
        store_kernel,
        name="store",
        out_shape=[jax.ShapeDtypeStruct(shape, BF16) for shape in shapes],
        in_specs=[vmem] * 4,
        out_specs=[hbm] * 4,
        scratch_shapes=[dma((2 + 2 * STORES,))],
        compiler_params=pltpu.CompilerParams(vmem_limit_bytes=2**20),
    )(*made)
    return mixed, token_grad, hidden_grad[None], output_grad[None]


def solution(mesh):
    return jax.shard_map(
        body,
        mesh=mesh,
        in_specs=(
            P("expert", "dp"),
            P("expert", "dp"),
            P("expert", None),
            P("expert", None),
            P("expert", "dp", None),
            P("expert", None, "dp"),
        ),
        out_specs=(
            P("expert", "dp"),
            P("expert", "dp"),
            P("expert", "dp", None),
            P("expert", None, "dp"),
        ),
        check_vma=False,
    )
```

```python
import functools

import jax
import jax.numpy as jnp
from jax import lax
from jax.experimental import pallas as pl
from jax.experimental.pallas import tpu as pltpu
from jax.sharding import PartitionSpec as P

MESH = pl.DeviceIdType.MESH
F32 = jnp.float32
BF16 = jnp.bfloat16
SLOTS = 16
EXPERTS = 32
CHUNKS = 8
PER = EXPERTS // CHUNKS
SPLIT = CHUNKS // 4
ROWS = PER * SLOTS
NX = 4
QUART = ROWS // NX
VMEM_LIMIT = 40 * 2**20
XP = 1
ZP = 1
AP = 1
DP = 2
RP = 1
LAST = (((1,), (1,)), ((), ()))
FIRST = (((0,), (0,)), ((), ()))

SCHEDULE = ('D0', 'D1', 'D2', 'D3', 'D4', 'D5', 'D6', 'D7', 'd0', 'p0', 't0', 'd1', 'p1', 'r0', 'd2', 'p2', 'r1', 'z0', 'd3', 'p3', 'r2', 'z1', 'g0', 'd4', 'p4', 'r3', 'z2', 'g1', 'd5', 'p5', 'r4', 'z3', 'g2', 'd6', 'p6', 'r5', 'z4', 'g3', 'd7', 'p7', 'r6', 'z5', 'g4', 'r7', 'z6', 'g5', 'z7', 'g6', 'g7', 'o0', 'h0', 'c0', 'c1', 'c2', 'c3', 'c4', 'c5', 'l0', 'c6', 'a0')


def kernel(
    routing_hbm,
    gate_hbm,
    tok_hbm,
    cot_hbm,
    w1_hbm,
    w2_hbm,
    mixed_sum,
    grad_sum,
    hgrad_ref,
    ograd_ref,
    last_rows,
    last_tables,
    routing_ref,
    gate_ref,
    tok_ref,
    cot_ref,
    w1,
    w2,
    place,
    whi,
    wlo,
    send,
    recv,
    part,
    xrecv,
    zsend,
    zrecv,
    act,
    rsend,
    rrecv,
    rows_t,
    place_t,
    whi_t,
    wlo_t,
    w_sem,
    d_send,
    d_recv,
    x_send,
    x_recv,
    z_send,
    z_recv,
    g_send,
    g_recv,
    r_send,
    r_recv,
):
    pairs = (
        (routing_hbm, routing_ref),
        (gate_hbm, gate_ref),
        (tok_hbm, tok_ref),
        (cot_hbm, cot_ref),
        (w1_hbm, w1),
        (w2_hbm, w2),
    )
    loads = [pltpu.make_async_copy(*pair, w_sem.at[i]) for i, pair in enumerate(pairs)]
    load1, load2 = loads[4:]
    for load in loads[:4]:
        load.start()
    dp = lax.axis_index("dp")
    me = lax.axis_index("expert")
    zh, x = dp // NX, dp % NX
    zl, y, core = me // 8, (me // 2) % 4, me % 2
    half = w2.shape[0]
    toks = tok_ref.shape[0]
    width = tok_ref.shape[1]
    z_peer = (1 - zh) * NX + x

    def x_peer(i):
        return zh * NX + (x + i) % NX

    def target(c, k):
        if SPLIT == 2:
            return k * 8 + ((y + 4 - c // 2) % 4) * 2 + (core + c) % 2
        return (k // 2) * 8 + ((y + 4 - c) % 4) * 2 + k % 2

    def origin(c, k):
        if SPLIT == 2:
            return k * 8 + ((y + c // 2) % 4) * 2 + (core + c) % 2
        return (k // 2) * 8 + ((y + c) % 4) * 2 + k % 2

    mine = zl if SPLIT == 2 else zl * 2 + core

    barrier = pltpu.get_barrier_semaphore()

    def greet(j, carry):
        pl.semaphore_signal(
            barrier, inc=1, device_id=(dp, (me + j) % EXPERTS), device_id_type=MESH
        )
        return carry

    lax.fori_loop(1, EXPERTS, greet, 0)
    for i in range(1, NX):
        pl.semaphore_signal(barrier, inc=1, device_id=(x_peer(i), me), device_id_type=MESH)
    pl.semaphore_signal(barrier, inc=1, device_id=(z_peer, me), device_id_type=MESH)

    load1.start()
    load2.start()
    loads[0].wait()
    loads[1].wait()

    ids = lax.broadcasted_iota(jnp.int32, (EXPERTS, toks), 0)
    member = jnp.zeros((EXPERTS, toks), F32)
    gates = jnp.zeros((EXPERTS, toks), F32)
    for k in range(routing_ref.shape[0]):
        hit = routing_ref[k : k + 1, :] == ids
        member = jnp.where(hit, 1.0, member)
        gates = jnp.where(hit, gate_ref[k : k + 1, :], gates)
    earlier = lax.broadcasted_iota(jnp.int32, (toks, toks), 0) < lax.broadcasted_iota(
        jnp.int32, (toks, toks), 1
    )
    earlier = jnp.where(earlier, 1.0, 0.0).astype(BF16)
    rank = jnp.dot(member.astype(BF16), earlier, preferred_element_type=F32)
    rank = jnp.where(member > 0.0, rank, -1.0).astype(BF16)
    slots = EXPERTS * SLOTS
    ids = lax.broadcasted_iota(jnp.int32, (1, EXPERTS), 1)
    place_of = (y + 4 - ((ids >> 1) & 3)) & 3
    if SPLIT == 2:
        place_of = (place_of * 2 + ((core + ids) & 1)) * PER + (ids >> 3)
    else:
        place_of = place_of * PER + (ids >> 3) * 2 + (ids & 1)
    spread = (
        lax.broadcasted_iota(jnp.int32, (slots, EXPERTS), 0) >> 4
    ) == place_of
    spread = jnp.where(spread, 1.0, 0.0).astype(BF16)
    within = lax.broadcasted_iota(jnp.int32, (slots, toks), 0) & (SLOTS - 1)
    hits = jnp.dot(spread, rank, preferred_element_type=F32) == within.astype(F32)
    high = gates.astype(BF16)
    low = (gates - high.astype(F32)).astype(BF16)
    place[...] = jnp.where(hits, 1.0, 0.0).astype(BF16)

    def gate_tables():
        whi[...] = jnp.where(
            hits, jnp.dot(spread, high, preferred_element_type=F32), 0.0
        ).astype(BF16)
        wlo[...] = jnp.where(
            hits, jnp.dot(spread, low, preferred_element_type=F32), 0.0
        ).astype(BF16)

    def pick_tokens(c):
        at = pl.ds(c * ROWS, ROWS)
        rows = jnp.dot(place[at, :], tok_ref[...], preferred_element_type=F32)
        send[c, :, 0] = rows.astype(BF16).reshape(PER, SLOTS, width)

    def pick_cotangents(c):
        at = pl.ds(c * ROWS, ROWS)
        rows = jnp.dot(whi[at, :], cot_ref[...], preferred_element_type=F32)
        rows += jnp.dot(wlo[at, :], cot_ref[...], preferred_element_type=F32)
        send[c, :, 1] = rows.astype(BF16).reshape(PER, SLOTS, width)

    def rows_part(ref, q, pieces):
        return ref if pieces == 1 else ref.at[q]

    def columns(q, pieces):
        return pl.ds(q * (3 * half // pieces), 3 * half // pieces)

    def dispatch_copy(c, j, q):
        k = (mine + j) % PER
        to = target(c, k)
        return pltpu.make_async_remote_copy(
            src_ref=rows_part(send.at[c, k], q, DP),
            dst_ref=rows_part(recv.at[c, mine], q, DP),
            send_sem=d_send.at[c, q, j],
            recv_sem=d_recv.at[c, q, mine],
            device_id=(dp, to),
            device_id_type=MESH,
        )

    def own_dispatch(q):
        return pltpu.make_async_copy(
            rows_part(send.at[0, mine], q, DP),
            rows_part(recv.at[0, mine], q, DP),
            d_recv.at[0, q, mine],
        )

    def return_copy(c, j, q):
        k = (mine + j) % PER
        to = origin(c, k)
        return pltpu.make_async_remote_copy(
            src_ref=rows_part(rsend.at[c, k], q, RP),
            dst_ref=rows_part(rrecv.at[c, mine], q, RP),
            send_sem=r_send.at[c, q, j],
            recv_sem=r_recv.at[c, q, mine],
            device_id=(dp, to),
            device_id_type=MESH,
        )

    def own_return(q):
        return pltpu.make_async_copy(
            rows_part(rsend.at[0, mine], q, RP),
            rows_part(rrecv.at[0, mine], q, RP),
            r_recv.at[0, q, mine],
        )

    def scatter_copy(c, i, q):
        to = (x + i) % NX
        return pltpu.make_async_remote_copy(
            src_ref=part.at[c, pl.ds(to * QUART, QUART), columns(q, XP)],
            dst_ref=xrecv.at[c, i - 1, :, columns(q, XP)],
            send_sem=x_send.at[c, i - 1, q],
            recv_sem=x_recv.at[c, i - 1, q],
            device_id=(x_peer(i), me),
            device_id_type=MESH,
        )

    def exchange_copy(c, q):
        return pltpu.make_async_remote_copy(
            src_ref=zsend.at[c, :, columns(q, ZP)],
            dst_ref=zrecv.at[c, :, columns(q, ZP)],
            send_sem=z_send.at[c, q],
            recv_sem=z_recv.at[c, q],
            device_id=(z_peer, me),
            device_id_type=MESH,
        )

    def gather_copy(c, i, owner, q):
        block = pl.ds(owner * QUART, QUART)
        return pltpu.make_async_remote_copy(
            src_ref=act.at[c, block, columns(q, AP)],
            dst_ref=act.at[c, block, columns(q, AP)],
            send_sem=g_send.at[c, i - 1, q],
            recv_sem=g_recv.at[c, i - 1, q],
            device_id=(x_peer(i), me),
            device_id_type=MESH,
        )

    def send_rows(c, q):
        if c == 0:
            own_dispatch(q).start()

        def one(j, carry):
            dispatch_copy(c, j, q).start()
            return carry

        lax.fori_loop(1 if c == 0 else 0, PER, one, 0)

    def start_dispatch(c):
        if c > 0:
            pick_tokens(c)
        if DP == 2:
            send_rows(c, 0)
        if c == 0:
            gate_tables()
            loads[3].wait()
        pick_cotangents(c)
        send_rows(c, DP - 1)

    def wait_rows(c, q):
        def one(k, carry):
            block = rows_part(recv.at[c, k], q, DP)
            pltpu.make_async_copy(block, block, d_recv.at[c, q, k]).wait()
            return carry

        lax.fori_loop(0, PER, one, 0)

    def wait_dispatch(c):
        pass

    def products(c):
        if c == 0:
            load1.wait()
            load2.wait()
        wait_rows(c, 0)
        tile = 512

        def hidden_tile(n, carry):
            at = pl.ds(pl.multiple_of(n * tile, tile), tile)
            part[c, :, at] = jnp.dot(
                recv[c, :, 0].reshape(ROWS, width), w1[:, at], preferred_element_type=F32
            ).astype(BF16)
            return carry

        lax.fori_loop(0, 2 * half // tile, hidden_tile, 0)
        if XP == 3:
            for q in range(2):
                for i in range(1, NX):
                    scatter_copy(c, i, q).start()
        if DP == 2:
            wait_rows(c, 1)

        def act_tile(n, carry):
            at = pl.ds(pl.multiple_of(n * tile, tile), tile)
            to = pl.ds(pl.multiple_of(2 * half + n * tile, tile), tile)
            part[c, :, to] = lax.dot_general(
                recv[c, :, 1].reshape(ROWS, width), w2[at, :], LAST, preferred_element_type=F32
            ).astype(BF16)
            return carry

        lax.fori_loop(0, half // tile, act_tile, 0)
        for q in range(2 if XP == 3 else 0, XP):
            for i in range(1, NX):
                scatter_copy(c, i, q).start()

    def reduce_x(c):
        for q in range(XP):
            for i in range(1, NX):
                scatter_copy(c, i, q).wait_recv()
        own = part[c, pl.ds(pl.multiple_of(x * QUART, QUART), QUART)].astype(F32)
        total = own + xrecv[c, 0].astype(F32)
        total += xrecv[c, 1].astype(F32)
        total += xrecv[c, 2].astype(F32)
        zsend[c] = total.astype(BF16)
        for q in range(ZP):
            exchange_copy(c, q).start()

    def activate(c):
        for q in range(ZP):
            exchange_copy(c, q).wait_recv()
        total = zsend[c].astype(F32) + zrecv[c].astype(F32)
        gate = total[:, :half]
        up = total[:, half : 2 * half]
        grad = total[:, 2 * half :]
        sig = jax.nn.sigmoid(gate)
        silu = gate * sig
        block = pl.ds(pl.multiple_of(x * QUART, QUART), QUART)
        act[c, block, 0:half] = (silu * up).astype(BF16)
        act[c, block, half : 2 * half] = (
            grad * up * sig * (1.0 + gate * (1.0 - sig))
        ).astype(BF16)
        act[c, block, 2 * half :] = (grad * silu).astype(BF16)
        for q in range(AP):
            for i in range(1, NX):
                gather_copy(c, i, x, q).start()

    def results(c):
        for q in range(AP):
            for i in range(1, NX):
                gather_copy(c, i, (x + NX - i) % NX, q).wait_recv()
        out = jnp.dot(act[c, :, 0:half], w2[...], preferred_element_type=F32)
        rsend[c, :, 0] = out.astype(BF16).reshape(PER, SLOTS, width)
        if RP == 2:
            send_results(c, 0)
        out = lax.dot_general(
            act[c, :, half:], w1[...], LAST, preferred_element_type=F32
        )
        rsend[c, :, 1] = out.astype(BF16).reshape(PER, SLOTS, width)
        send_results(c, RP - 1)

    def send_results(c, q):
        if c == 0:
            own_return(q).start()

        def one(j, carry):
            return_copy(c, j, q).start()
            return carry

        lax.fori_loop(1 if c == 0 else 0, PER, one, 0)

    def transposes():
        place_t[...] = place[...].T
        whi_t[...] = whi[...].T
        wlo_t[...] = wlo[...].T

    def wait_results(c):
        def arrived(k, carry):
            for q in range(RP):
                block = rows_part(rrecv.at[c, k], q, RP)
                pltpu.make_async_copy(block, block, r_recv.at[c, q, k]).wait()
            return carry

        lax.fori_loop(0, PER, arrived, 0)

    def combine(c):
        wait_results(c)
        at = pl.ds(c * ROWS, ROWS)
        back = rrecv[c, :, 0].reshape(ROWS, width)
        mixed = jnp.dot(whi_t[:, at], back, preferred_element_type=F32)
        mixed += jnp.dot(wlo_t[:, at], back, preferred_element_type=F32)
        back = rrecv[c, :, 1].reshape(ROWS, width)
        grads = jnp.dot(place_t[:, at], back, preferred_element_type=F32)
        if c > 0:
            mixed += mixed_sum[...]
            grads += grad_sum[...]
        mixed_sum[...] = mixed
        grad_sum[...] = grads

    def hand_over(_):
        at = pl.ds((CHUNKS - 1) * ROWS, ROWS)
        for n, table in enumerate((whi_t, wlo_t, place_t)):
            last_tables[n] = table[:, at]

    def last_arrivals(_):
        wait_results(CHUNKS - 1)
        for q in range(2):
            last_rows[q] = rrecv[CHUNKS - 1, :, q].reshape(ROWS, width)

    loads[2].wait()
    pick_tokens(0)
    pl.semaphore_wait(barrier, EXPERTS - 1 + NX)

    run = {
        "D": start_dispatch,
        "d": wait_dispatch,
        "p": products,
        "r": reduce_x,
        "z": activate,
        "g": results,
    }
    def output_gradient(_):
        tile = 256

        def one(n, carry):
            at = pl.ds(pl.multiple_of(n * tile, tile), tile)
            ograd_ref[at, :] = lax.dot_general(
                act[:, :, at].reshape(slots, tile),
                recv[:, :, 1].reshape(slots, width),
                FIRST,
                preferred_element_type=F32,
            ).astype(BF16)
            return carry

        lax.fori_loop(0, half // tile, one, 0)

    def hidden_gradient(_):
        tile = 256
        rows_t[...] = recv[:, :, 0].reshape(slots, width).T

        def one(n, carry):
            at = pl.ds(pl.multiple_of(n * tile, tile), tile)
            cots = act[:, :, pl.ds(pl.multiple_of(half + n * tile, tile), tile)]
            hgrad_ref[:, at] = jnp.dot(
                rows_t[...], cots.reshape(slots, tile), preferred_element_type=F32
            ).astype(BF16)
            return carry

        lax.fori_loop(0, 2 * half // tile, one, 0)

    run["t"] = lambda _: transposes()
    run["o"] = output_gradient
    run["h"] = hidden_gradient
    run["c"] = combine
    run["l"] = hand_over
    run["a"] = last_arrivals
    for step in SCHEDULE:
        run[step[0]](int(step[1]))

    for c in range(CHUNKS):

        def left(j, carry):
            for q in range(DP):
                dispatch_copy(c, j, q).wait_send()
            for q in range(RP):
                return_copy(c, j, q).wait_send()
            return carry

        lax.fori_loop(1 if c == 0 else 0, PER, left, 0)
        for i in range(1, NX):
            for q in range(XP):
                scatter_copy(c, i, q).wait_send()
            for q in range(AP):
                gather_copy(c, i, x, q).wait_send()
        for q in range(ZP):
            exchange_copy(c, q).wait_send()


def store_kernel(
    mixed_sum,
    grad_sum,
    hgrad,
    ograd,
    rows,
    tables,
    mixed_out,
    tgrad_out,
    hgrad_out,
    ograd_out,
    mixed,
    tgrad,
    sem,
):
    pairs = ((hgrad, hgrad_out), (ograd, ograd_out), (mixed, mixed_out), (tgrad, tgrad_out))
    copies = [pltpu.make_async_copy(*pair, sem.at[i]) for i, pair in enumerate(pairs)]
    copies[0].start()
    copies[1].start()
    total = mixed_sum[...] + jnp.dot(tables[0], rows[0], preferred_element_type=F32)
    total += jnp.dot(tables[1], rows[0], preferred_element_type=F32)
    mixed[...] = total.astype(BF16)
    copies[2].start()
    total = grad_sum[...] + jnp.dot(tables[2], rows[1], preferred_element_type=F32)
    tgrad[...] = total.astype(BF16)
    copies[3].start()
    for copy in copies:
        copy.wait()


def body(tokens, cotangent, routing, gate_values, hidden_weight, output_weight):
    toks, width = tokens.shape
    half = output_weight.shape[1]
    wide = 3 * half
    dma = pltpu.SemaphoreType.DMA
    vmem = pl.BlockSpec(memory_space=pltpu.VMEM)
    hbm = pl.BlockSpec(memory_space=pltpu.HBM)
    shapes = ((toks, width), (toks, width), (width, 2 * half), (half, width))
    slots = EXPERTS * SLOTS
    made = pl.pallas_call(
        kernel,
        name="moe_layer",
        out_shape=[pltpu.VMEM(shape, F32) for shape in shapes[:2]]
        + [pltpu.VMEM(shape, BF16) for shape in shapes[2:]]
        + [pltpu.VMEM((2, ROWS, width), BF16), pltpu.VMEM((3, toks, ROWS), BF16)],
        in_specs=[hbm] * 6,
        out_specs=[vmem] * 6,
        scratch_shapes=[
            pltpu.VMEM(routing.shape[::-1], jnp.int32),
            pltpu.VMEM(routing.shape[::-1], F32),
            pltpu.VMEM((toks, width), BF16),
            pltpu.VMEM((toks, width), BF16),
            pltpu.VMEM((width, 2 * half), BF16),
            pltpu.VMEM((half, width), BF16),
            pltpu.VMEM((slots, toks), BF16),
            pltpu.VMEM((slots, toks), BF16),
            pltpu.VMEM((slots, toks), BF16),
            pltpu.VMEM((CHUNKS, PER, 2, SLOTS, width), BF16),
            pltpu.VMEM((CHUNKS, PER, 2, SLOTS, width), BF16),
            pltpu.VMEM((CHUNKS, ROWS, wide), BF16),
            pltpu.VMEM((CHUNKS, NX - 1, QUART, wide), BF16),
            pltpu.VMEM((CHUNKS, QUART, wide), BF16),
            pltpu.VMEM((CHUNKS, QUART, wide), BF16),
            pltpu.VMEM((CHUNKS, ROWS, wide), BF16),
            pltpu.VMEM((CHUNKS, PER, 2, SLOTS, width), BF16),
            pltpu.VMEM((CHUNKS, PER, 2, SLOTS, width), BF16),
            pltpu.VMEM((width, slots), BF16),
            pltpu.VMEM((toks, slots), BF16),
            pltpu.VMEM((toks, slots), BF16),
            pltpu.VMEM((toks, slots), BF16),
            dma((6,)),
            dma((CHUNKS, DP, PER)),
            dma((CHUNKS, DP, PER)),
            dma((CHUNKS, NX - 1, XP)),
            dma((CHUNKS, NX - 1, XP)),
            dma((CHUNKS, ZP)),
            dma((CHUNKS, ZP)),
            dma((CHUNKS, NX - 1, AP)),
            dma((CHUNKS, NX - 1, AP)),
            dma((CHUNKS, RP, PER)),
            dma((CHUNKS, RP, PER)),
        ],
        compiler_params=pltpu.CompilerParams(
            collective_id=0, has_side_effects=True, vmem_limit_bytes=VMEM_LIMIT
        ),
    )(
        *[
            pltpu.with_memory_space_constraint(value, pltpu.HBM)
            for value in (
                routing.T,
                gate_values.T,
                tokens,
                cotangent,
                hidden_weight[0],
                output_weight[0],
            )
        ]
    )
    made = [pltpu.with_memory_space_constraint(value, pltpu.VMEM) for value in made]
    mixed, token_grad, hidden_grad, output_grad = pl.pallas_call(
        store_kernel,
        name="store",
        out_shape=[jax.ShapeDtypeStruct(shape, BF16) for shape in shapes],
        in_specs=[vmem] * 6,
        out_specs=[hbm] * 4,
        scratch_shapes=[
            pltpu.VMEM((toks, width), BF16),
            pltpu.VMEM((toks, width), BF16),
            dma((4,)),
        ],
        compiler_params=pltpu.CompilerParams(vmem_limit_bytes=8 * 2**20),
    )(*made)
    return mixed, token_grad, hidden_grad[None], output_grad[None]


def solution(mesh):
    return jax.shard_map(
        body,
        mesh=mesh,
        in_specs=(
            P("expert", "dp"),
            P("expert", "dp"),
            P("expert", None),
            P("expert", None),
            P("expert", "dp", None),
            P("expert", None, "dp"),
        ),
        out_specs=(
            P("expert", "dp"),
            P("expert", "dp"),
            P("expert", "dp", None),
            P("expert", None, "dp"),
        ),
        check_vma=False,
    )
```

```python
import functools

import jax
import jax.numpy as jnp
from jax import lax
from jax.experimental import pallas as pl
from jax.experimental.pallas import tpu as pltpu
from jax.sharding import PartitionSpec as P

MESH = pl.DeviceIdType.MESH
F32 = jnp.float32
BF16 = jnp.bfloat16
SLOTS = 16
EXPERTS = 32
CHUNKS = 8
PER = EXPERTS // CHUNKS
SPLIT = CHUNKS // 4
ROWS = PER * SLOTS
NX = 4
QUART = ROWS // NX
VMEM_LIMIT = 40 * 2**20
XP = 1
ZP = 1
AP = 1
DP = 2
RP = 1
LAST = (((1,), (1,)), ((), ()))
FIRST = (((0,), (0,)), ((), ()))

SCHEDULE = ('D0', 'D1', 'D2', 'D3', 'D4', 'D5', 'D6', 'D7', 'd0', 'p0', 't0', 'd1', 'p1', 'r0', 'd2', 'p2', 'r1', 'z0', 'd3', 'p3', 'r2', 'z1', 'g0', 'd4', 'p4', 'r3', 'z2', 'g1', 'd5', 'p5', 'r4', 'z3', 'g2', 'd6', 'p6', 'r5', 'z4', 'g3', 'd7', 'p7', 'r6', 'z5', 'g4', 'r7', 'z6', 'g5', 'z7', 'g6', 'g7', 'o0', 'h0', 'c0', 'c1', 'c2', 'c3', 'c4', 'c5', 'l0', 'c6', 'a0')


def kernel(
    routing_hbm,
    gate_hbm,
    tok_hbm,
    cot_hbm,
    w1_hbm,
    w2_hbm,
    mixed_sum,
    grad_sum,
    hgrad_ref,
    ograd_ref,
    last_rows,
    last_tables,
    routing_ref,
    gate_ref,
    tok_ref,
    cot_ref,
    w1,
    w2,
    place,
    whi,
    wlo,
    send,
    recv,
    part,
    xrecv,
    zsend,
    zrecv,
    act,
    rsend,
    rrecv,
    rows_t,
    place_t,
    whi_t,
    wlo_t,
    ready,
    w_sem,
    d_send,
    d_recv,
    x_send,
    x_recv,
    z_send,
    z_recv,
    g_send,
    g_recv,
    r_send,
    r_recv,
):
    pairs = (
        (routing_hbm, routing_ref),
        (gate_hbm, gate_ref),
        (tok_hbm, tok_ref),
        (cot_hbm, cot_ref),
        (w1_hbm, w1),
        (w2_hbm, w2),
    )
    loads = [pltpu.make_async_copy(*pair, w_sem.at[i]) for i, pair in enumerate(pairs)]
    load1, load2 = loads[4:]
    for load in loads[:4]:
        load.start()
    dp = lax.axis_index("dp")
    me = lax.axis_index("expert")
    zh, x = dp // NX, dp % NX
    zl, y, core = me // 8, (me // 2) % 4, me % 2
    half = w2.shape[0]
    toks = tok_ref.shape[0]
    width = tok_ref.shape[1]
    z_peer = (1 - zh) * NX + x

    def x_peer(i):
        return zh * NX + (x + i) % NX

    def target(c, k):
        if SPLIT == 2:
            return k * 8 + ((y + 4 - c // 2) % 4) * 2 + (core + c) % 2
        return (k // 2) * 8 + ((y + 4 - c) % 4) * 2 + k % 2

    def origin(c, k):
        if SPLIT == 2:
            return k * 8 + ((y + c // 2) % 4) * 2 + (core + c) % 2
        return (k // 2) * 8 + ((y + c) % 4) * 2 + k % 2

    mine = zl if SPLIT == 2 else zl * 2 + core

    barrier = pltpu.get_barrier_semaphore()

    def greet(j, carry):
        pl.semaphore_signal(
            barrier, inc=1, device_id=(dp, (me + j) % EXPERTS), device_id_type=MESH
        )
        return carry

    lax.fori_loop(1, EXPERTS, greet, 0)
    for i in range(1, NX):
        pl.semaphore_signal(barrier, inc=1, device_id=(x_peer(i), me), device_id_type=MESH)

    @pl.when(zh == 0)
    def greet_upper():
        pl.semaphore_signal(
            barrier, inc=1, device_id=(z_peer, me), device_id_type=MESH
        )


    load1.start()
    load2.start()
    loads[0].wait()
    loads[1].wait()

    ids = lax.broadcasted_iota(jnp.int32, (EXPERTS, toks), 0)
    member = jnp.zeros((EXPERTS, toks), F32)
    gates = jnp.zeros((EXPERTS, toks), F32)
    for k in range(routing_ref.shape[0]):
        hit = routing_ref[k : k + 1, :] == ids
        member = jnp.where(hit, 1.0, member)
        gates = jnp.where(hit, gate_ref[k : k + 1, :], gates)
    earlier = lax.broadcasted_iota(jnp.int32, (toks, toks), 0) < lax.broadcasted_iota(
        jnp.int32, (toks, toks), 1
    )
    earlier = jnp.where(earlier, 1.0, 0.0).astype(BF16)
    rank = jnp.dot(member.astype(BF16), earlier, preferred_element_type=F32)
    rank = jnp.where(member > 0.0, rank, -1.0).astype(BF16)
    slots = EXPERTS * SLOTS
    ids = lax.broadcasted_iota(jnp.int32, (1, EXPERTS), 1)
    place_of = (y + 4 - ((ids >> 1) & 3)) & 3
    if SPLIT == 2:
        place_of = (place_of * 2 + ((core + ids) & 1)) * PER + (ids >> 3)
    else:
        place_of = place_of * PER + (ids >> 3) * 2 + (ids & 1)
    spread = (
        lax.broadcasted_iota(jnp.int32, (slots, EXPERTS), 0) >> 4
    ) == place_of
    spread = jnp.where(spread, 1.0, 0.0).astype(BF16)
    within = lax.broadcasted_iota(jnp.int32, (slots, toks), 0) & (SLOTS - 1)
    hits = jnp.dot(spread, rank, preferred_element_type=F32) == within.astype(F32)
    high = gates.astype(BF16)
    low = (gates - high.astype(F32)).astype(BF16)
    place[...] = jnp.where(hits, 1.0, 0.0).astype(BF16)

    def gate_tables():
        whi[...] = jnp.where(
            hits, jnp.dot(spread, high, preferred_element_type=F32), 0.0
        ).astype(BF16)
        wlo[...] = jnp.where(
            hits, jnp.dot(spread, low, preferred_element_type=F32), 0.0
        ).astype(BF16)

    def pick_tokens(c):
        at = pl.ds(c * ROWS, ROWS)
        rows = jnp.dot(place[at, :], tok_ref[...], preferred_element_type=F32)
        send[c, :, 0] = rows.astype(BF16).reshape(PER, SLOTS, width)

    def pick_cotangents(c):
        at = pl.ds(c * ROWS, ROWS)
        rows = jnp.dot(whi[at, :], cot_ref[...], preferred_element_type=F32)
        rows += jnp.dot(wlo[at, :], cot_ref[...], preferred_element_type=F32)
        send[c, :, 1] = rows.astype(BF16).reshape(PER, SLOTS, width)

    def rows_part(ref, q, pieces):
        return ref if pieces == 1 else ref.at[q]

    def columns(q, pieces):
        return pl.ds(q * (3 * half // pieces), 3 * half // pieces)

    def dispatch_copy(c, j, q):
        k = (mine + j) % PER
        to = target(c, k)
        return pltpu.make_async_remote_copy(
            src_ref=rows_part(send.at[c, k], q, DP),
            dst_ref=rows_part(recv.at[c, mine], q, DP),
            send_sem=d_send.at[c, q, j],
            recv_sem=d_recv.at[c, q, mine],
            device_id=(dp, to),
            device_id_type=MESH,
        )

    def own_dispatch(q):
        return pltpu.make_async_copy(
            rows_part(send.at[0, mine], q, DP),
            rows_part(recv.at[0, mine], q, DP),
            d_recv.at[0, q, mine],
        )

    def return_copy(c, j, q):
        k = (mine + j) % PER
        to = origin(c, k)
        return pltpu.make_async_remote_copy(
            src_ref=rows_part(rsend.at[c, k], q, RP),
            dst_ref=rows_part(rrecv.at[c, mine], q, RP),
            send_sem=r_send.at[c, q, j],
            recv_sem=r_recv.at[c, q, mine],
            device_id=(dp, to),
            device_id_type=MESH,
        )

    def own_return(q):
        return pltpu.make_async_copy(
            rows_part(rsend.at[0, mine], q, RP),
            rows_part(rrecv.at[0, mine], q, RP),
            r_recv.at[0, q, mine],
        )

    def scatter_copy(c, i, q):
        to = (x + i) % NX
        return pltpu.make_async_remote_copy(
            src_ref=part.at[c, pl.ds(to * QUART, QUART), columns(q, XP)],
            dst_ref=xrecv.at[c, i - 1, :, columns(q, XP)],
            send_sem=x_send.at[c, i - 1, q],
            recv_sem=x_recv.at[c, i - 1, q],
            device_id=(x_peer(i), me),
            device_id_type=MESH,
        )

    def exchange_copy(c, q):
        return pltpu.make_async_remote_copy(
            src_ref=zsend.at[c, :, columns(q, ZP)],
            dst_ref=zrecv.at[c, :, columns(q, ZP)],
            send_sem=z_send.at[c, q],
            recv_sem=z_recv.at[c, q],
            device_id=(z_peer, me),
            device_id_type=MESH,
        )

    def gather_copy(c, i, owner, q):
        block = pl.ds(owner * QUART, QUART)
        return pltpu.make_async_remote_copy(
            src_ref=act.at[c, block, columns(q, AP)],
            dst_ref=act.at[c, block, columns(q, AP)],
            send_sem=g_send.at[c, i - 1, q],
            recv_sem=g_recv.at[c, i - 1, q],
            device_id=(x_peer(i), me),
            device_id_type=MESH,
        )

    def send_rows(c, q):
        if c == 0:
            own_dispatch(q).start()

        def one(j, carry):
            dispatch_copy(c, j, q).start()
            return carry

        lax.fori_loop(1 if c == 0 else 0, PER, one, 0)

    def start_dispatch(c):
        if c > 0:
            pick_tokens(c)
        if DP == 2:
            send_rows(c, 0)
        if c == 0:
            gate_tables()
            loads[3].wait()
        pick_cotangents(c)
        send_rows(c, DP - 1)

    def wait_rows(c, q):
        def one(k, carry):
            block = rows_part(recv.at[c, k], q, DP)
            pltpu.make_async_copy(block, block, d_recv.at[c, q, k]).wait()
            return carry

        lax.fori_loop(0, PER, one, 0)

    def wait_dispatch(c):
        pass

    def products(c):
        if c == 0:
            load1.wait()
            load2.wait()
        wait_rows(c, 0)
        tile = 512

        def hidden_tile(n, carry):
            at = pl.ds(pl.multiple_of(n * tile, tile), tile)
            part[c, :, at] = jnp.dot(
                recv[c, :, 0].reshape(ROWS, width), w1[:, at], preferred_element_type=F32
            ).astype(BF16)
            return carry

        lax.fori_loop(0, 2 * half // tile, hidden_tile, 0)
        if XP == 3:
            for q in range(2):
                for i in range(1, NX):
                    scatter_copy(c, i, q).start()
        if DP == 2:
            wait_rows(c, 1)

        def act_tile(n, carry):
            at = pl.ds(pl.multiple_of(n * tile, tile), tile)
            to = pl.ds(pl.multiple_of(2 * half + n * tile, tile), tile)
            part[c, :, to] = lax.dot_general(
                recv[c, :, 1].reshape(ROWS, width), w2[at, :], LAST, preferred_element_type=F32
            ).astype(BF16)
            return carry

        lax.fori_loop(0, half // tile, act_tile, 0)
        for q in range(2 if XP == 3 else 0, XP):
            for i in range(1, NX):
                scatter_copy(c, i, q).start()

    def reduce_x(c):
        if c == 0:

            @pl.when(zh == 0)
            def upper_is_in():
                pl.semaphore_wait(ready, 1)

        for q in range(XP):
            for i in range(1, NX):
                scatter_copy(c, i, q).wait_recv()
        own = part[c, pl.ds(pl.multiple_of(x * QUART, QUART), QUART)].astype(F32)
        total = own + xrecv[c, 0].astype(F32)
        total += xrecv[c, 1].astype(F32)
        total += xrecv[c, 2].astype(F32)
        zsend[c] = total.astype(BF16)
        for q in range(ZP):
            exchange_copy(c, q).start()

    def activate(c):
        for q in range(ZP):
            exchange_copy(c, q).wait_recv()
        total = zsend[c].astype(F32) + zrecv[c].astype(F32)
        gate = total[:, :half]
        up = total[:, half : 2 * half]
        grad = total[:, 2 * half :]
        sig = jax.nn.sigmoid(gate)
        silu = gate * sig
        block = pl.ds(pl.multiple_of(x * QUART, QUART), QUART)
        act[c, block, 0:half] = (silu * up).astype(BF16)
        act[c, block, half : 2 * half] = (
            grad * up * sig * (1.0 + gate * (1.0 - sig))
        ).astype(BF16)
        act[c, block, 2 * half :] = (grad * silu).astype(BF16)
        for q in range(AP):
            for i in range(1, NX):
                gather_copy(c, i, x, q).start()

    def results(c):
        for q in range(AP):
            for i in range(1, NX):
                gather_copy(c, i, (x + NX - i) % NX, q).wait_recv()
        out = jnp.dot(act[c, :, 0:half], w2[...], preferred_element_type=F32)
        rsend[c, :, 0] = out.astype(BF16).reshape(PER, SLOTS, width)
        if RP == 2:
            send_results(c, 0)
        out = lax.dot_general(
            act[c, :, half:], w1[...], LAST, preferred_element_type=F32
        )
        rsend[c, :, 1] = out.astype(BF16).reshape(PER, SLOTS, width)
        send_results(c, RP - 1)

    def send_results(c, q):
        if c == 0:
            own_return(q).start()

        def one(j, carry):
            return_copy(c, j, q).start()
            return carry

        lax.fori_loop(1 if c == 0 else 0, PER, one, 0)

    def transposes():
        place_t[...] = place[...].T
        whi_t[...] = whi[...].T
        wlo_t[...] = wlo[...].T

    def wait_results(c):
        def arrived(k, carry):
            for q in range(RP):
                block = rows_part(rrecv.at[c, k], q, RP)
                pltpu.make_async_copy(block, block, r_recv.at[c, q, k]).wait()
            return carry

        lax.fori_loop(0, PER, arrived, 0)

    def combine(c):
        wait_results(c)
        at = pl.ds(c * ROWS, ROWS)
        back = rrecv[c, :, 0].reshape(ROWS, width)
        mixed = jnp.dot(whi_t[:, at], back, preferred_element_type=F32)
        mixed += jnp.dot(wlo_t[:, at], back, preferred_element_type=F32)
        back = rrecv[c, :, 1].reshape(ROWS, width)
        grads = jnp.dot(place_t[:, at], back, preferred_element_type=F32)
        if c > 0:
            mixed += mixed_sum[...]
            grads += grad_sum[...]
        mixed_sum[...] = mixed
        grad_sum[...] = grads

    def hand_over(_):
        at = pl.ds((CHUNKS - 1) * ROWS, ROWS)
        for n, table in enumerate((whi_t, wlo_t, place_t)):
            last_tables[n] = table[:, at]

    def last_arrivals(_):
        wait_results(CHUNKS - 1)
        for q in range(2):
            last_rows[q] = rrecv[CHUNKS - 1, :, q].reshape(ROWS, width)

    loads[2].wait()
    pick_tokens(0)
    pl.semaphore_wait(barrier, EXPERTS - 1 + NX - 1 + zh)

    @pl.when(zh == 1)
    def answer():
        pl.semaphore_signal(ready, inc=1, device_id=(z_peer, me), device_id_type=MESH)


    run = {
        "D": start_dispatch,
        "d": wait_dispatch,
        "p": products,
        "r": reduce_x,
        "z": activate,
        "g": results,
    }
    def output_gradient(_):
        tile = 256

        def one(n, carry):
            at = pl.ds(pl.multiple_of(n * tile, tile), tile)
            ograd_ref[at, :] = lax.dot_general(
                act[:, :, at].reshape(slots, tile),
                recv[:, :, 1].reshape(slots, width),
                FIRST,
                preferred_element_type=F32,
            ).astype(BF16)
            return carry

        lax.fori_loop(0, half // tile, one, 0)

    def hidden_gradient(_):
        tile = 256
        rows_t[...] = recv[:, :, 0].reshape(slots, width).T

        def one(n, carry):
            at = pl.ds(pl.multiple_of(n * tile, tile), tile)
            cots = act[:, :, pl.ds(pl.multiple_of(half + n * tile, tile), tile)]
            hgrad_ref[:, at] = jnp.dot(
                rows_t[...], cots.reshape(slots, tile), preferred_element_type=F32
            ).astype(BF16)
            return carry

        lax.fori_loop(0, 2 * half // tile, one, 0)

    run["t"] = lambda _: transposes()
    run["o"] = output_gradient
    run["h"] = hidden_gradient
    run["c"] = combine
    run["l"] = hand_over
    run["a"] = last_arrivals
    for step in SCHEDULE:
        run[step[0]](int(step[1]))

    for c in range(CHUNKS):

        def left(j, carry):
            for q in range(DP):
                dispatch_copy(c, j, q).wait_send()
            for q in range(RP):
                return_copy(c, j, q).wait_send()
            return carry

        lax.fori_loop(1 if c == 0 else 0, PER, left, 0)
        for i in range(1, NX):
            for q in range(XP):
                scatter_copy(c, i, q).wait_send()
            for q in range(AP):
                gather_copy(c, i, x, q).wait_send()
        for q in range(ZP):
            exchange_copy(c, q).wait_send()


def store_kernel(
    mixed_sum,
    grad_sum,
    hgrad,
    ograd,
    rows,
    tables,
    mixed_out,
    tgrad_out,
    hgrad_out,
    ograd_out,
    mixed,
    tgrad,
    sem,
):
    pairs = ((hgrad, hgrad_out), (ograd, ograd_out), (mixed, mixed_out), (tgrad, tgrad_out))
    copies = [pltpu.make_async_copy(*pair, sem.at[i]) for i, pair in enumerate(pairs)]
    copies[0].start()
    copies[1].start()
    total = mixed_sum[...] + jnp.dot(tables[0], rows[0], preferred_element_type=F32)
    total += jnp.dot(tables[1], rows[0], preferred_element_type=F32)
    mixed[...] = total.astype(BF16)
    copies[2].start()
    total = grad_sum[...] + jnp.dot(tables[2], rows[1], preferred_element_type=F32)
    tgrad[...] = total.astype(BF16)
    copies[3].start()
    for copy in copies:
        copy.wait()


def body(tokens, cotangent, routing, gate_values, hidden_weight, output_weight):
    toks, width = tokens.shape
    half = output_weight.shape[1]
    wide = 3 * half
    dma = pltpu.SemaphoreType.DMA
    vmem = pl.BlockSpec(memory_space=pltpu.VMEM)
    hbm = pl.BlockSpec(memory_space=pltpu.HBM)
    shapes = ((toks, width), (toks, width), (width, 2 * half), (half, width))
    slots = EXPERTS * SLOTS
    made = pl.pallas_call(
        kernel,
        name="moe_layer",
        out_shape=[pltpu.VMEM(shape, F32) for shape in shapes[:2]]
        + [pltpu.VMEM(shape, BF16) for shape in shapes[2:]]
        + [pltpu.VMEM((2, ROWS, width), BF16), pltpu.VMEM((3, toks, ROWS), BF16)],
        in_specs=[hbm] * 6,
        out_specs=[vmem] * 6,
        scratch_shapes=[
            pltpu.VMEM(routing.shape[::-1], jnp.int32),
            pltpu.VMEM(routing.shape[::-1], F32),
            pltpu.VMEM((toks, width), BF16),
            pltpu.VMEM((toks, width), BF16),
            pltpu.VMEM((width, 2 * half), BF16),
            pltpu.VMEM((half, width), BF16),
            pltpu.VMEM((slots, toks), BF16),
            pltpu.VMEM((slots, toks), BF16),
            pltpu.VMEM((slots, toks), BF16),
            pltpu.VMEM((CHUNKS, PER, 2, SLOTS, width), BF16),
            pltpu.VMEM((CHUNKS, PER, 2, SLOTS, width), BF16),
            pltpu.VMEM((CHUNKS, ROWS, wide), BF16),
            pltpu.VMEM((CHUNKS, NX - 1, QUART, wide), BF16),
            pltpu.VMEM((CHUNKS, QUART, wide), BF16),
            pltpu.VMEM((CHUNKS, QUART, wide), BF16),
            pltpu.VMEM((CHUNKS, ROWS, wide), BF16),
            pltpu.VMEM((CHUNKS, PER, 2, SLOTS, width), BF16),
            pltpu.VMEM((CHUNKS, PER, 2, SLOTS, width), BF16),
            pltpu.VMEM((width, slots), BF16),
            pltpu.VMEM((toks, slots), BF16),
            pltpu.VMEM((toks, slots), BF16),
            pltpu.VMEM((toks, slots), BF16),
            pltpu.SemaphoreType.REGULAR,
            dma((6,)),
            dma((CHUNKS, DP, PER)),
            dma((CHUNKS, DP, PER)),
            dma((CHUNKS, NX - 1, XP)),
            dma((CHUNKS, NX - 1, XP)),
            dma((CHUNKS, ZP)),
            dma((CHUNKS, ZP)),
            dma((CHUNKS, NX - 1, AP)),
            dma((CHUNKS, NX - 1, AP)),
            dma((CHUNKS, RP, PER)),
            dma((CHUNKS, RP, PER)),
        ],
        compiler_params=pltpu.CompilerParams(
            collective_id=0, has_side_effects=True, vmem_limit_bytes=VMEM_LIMIT
        ),
    )(
        *[
            pltpu.with_memory_space_constraint(value, pltpu.HBM)
            for value in (
                routing.T,
                gate_values.T,
                tokens,
                cotangent,
                hidden_weight[0],
                output_weight[0],
            )
        ]
    )
    made = [pltpu.with_memory_space_constraint(value, pltpu.VMEM) for value in made]
    mixed, token_grad, hidden_grad, output_grad = pl.pallas_call(
        store_kernel,
        name="store",
        out_shape=[jax.ShapeDtypeStruct(shape, BF16) for shape in shapes],
        in_specs=[vmem] * 6,
        out_specs=[hbm] * 4,
        scratch_shapes=[
            pltpu.VMEM((toks, width), BF16),
            pltpu.VMEM((toks, width), BF16),
            dma((4,)),
        ],
        compiler_params=pltpu.CompilerParams(vmem_limit_bytes=8 * 2**20),
    )(*made)
    return mixed, token_grad, hidden_grad[None], output_grad[None]


def solution(mesh):
    return jax.shard_map(
        body,
        mesh=mesh,
        in_specs=(
            P("expert", "dp"),
            P("expert", "dp"),
            P("expert", None),
            P("expert", None),
            P("expert", "dp", None),
            P("expert", None, "dp"),
        ),
        out_specs=(
            P("expert", "dp"),
            P("expert", "dp"),
            P("expert", "dp", None),
            P("expert", None, "dp"),
        ),
        check_vma=False,
    )
```

```python
import functools

import jax
import jax.numpy as jnp
from jax import lax
from jax.experimental import pallas as pl
from jax.experimental.pallas import tpu as pltpu
from jax.sharding import PartitionSpec as P

MESH = pl.DeviceIdType.MESH
F32 = jnp.float32
BF16 = jnp.bfloat16
SLOTS = 16
EXPERTS = 32
CHUNKS = 8
PER = EXPERTS // CHUNKS
SPLIT = CHUNKS // 4
ROWS = PER * SLOTS
OWN = 6
NX = 4
QUART = ROWS // NX
VMEM_LIMIT = 40 * 2**20
XP = 1
ZP = 1
AP = 1
DP = 2
RP = 1
LAST = (((1,), (1,)), ((), ()))
FIRST = (((0,), (0,)), ((), ()))

SCHEDULE = ('D0', 'D1', 'D2', 'D3', 'D4', 'D5', 'D6', 'D7', 'd0', 'p0', 't0', 'd1', 'p1', 'r0', 'd2', 'p2', 'r1', 'z0', 'd3', 'p3', 'r2', 'z1', 'g0', 'd4', 'p4', 'r3', 'z2', 'g1', 'd5', 'p5', 'r4', 'z3', 'g2', 'd6', 'p6', 'r5', 'z4', 'g3', 'd7', 'p7', 'r6', 'z5', 'g4', 'r7', 'z6', 'g5', 'z7', 'g6', 'g7', 'o0', 'h0', 'c0', 'c1', 'c2', 'c3', 'c4', 'c5', 'l0', 'c6', 'a0')


def kernel(
    routing_hbm,
    gate_hbm,
    tok_hbm,
    cot_hbm,
    w1_hbm,
    w2_hbm,
    mixed_sum,
    grad_sum,
    hgrad_ref,
    ograd_ref,
    last_rows,
    last_tables,
    routing_ref,
    gate_ref,
    tok_ref,
    cot_ref,
    w1,
    w2,
    place,
    whi,
    wlo,
    send,
    recv,
    part,
    xrecv,
    zsend,
    zrecv,
    act,
    rsend,
    rrecv,
    rows_t,
    place_t,
    whi_t,
    wlo_t,
    ready,
    w_sem,
    d_send,
    d_recv,
    x_send,
    x_recv,
    z_send,
    z_recv,
    g_send,
    g_recv,
    r_send,
    r_recv,
):
    pairs = (
        (routing_hbm, routing_ref),
        (gate_hbm, gate_ref),
        (tok_hbm, tok_ref),
        (cot_hbm, cot_ref),
        (w1_hbm, w1),
        (w2_hbm, w2),
    )
    loads = [pltpu.make_async_copy(*pair, w_sem.at[i]) for i, pair in enumerate(pairs)]
    load1, load2 = loads[4:]
    for load in loads[:4]:
        load.start()
    dp = lax.axis_index("dp")
    me = lax.axis_index("expert")
    zh, x = dp // NX, dp % NX
    zl, y, core = me // 8, (me // 2) % 4, me % 2
    half = w2.shape[0]
    toks = tok_ref.shape[0]
    width = tok_ref.shape[1]
    z_peer = (1 - zh) * NX + x

    def x_peer(i):
        return zh * NX + (x + i) % NX

    def target(c, k):
        if SPLIT == 2:
            return k * 8 + ((y + 3 - c // 2) % 4) * 2 + (core + c) % 2
        return (k // 2) * 8 + ((y + 4 - c) % 4) * 2 + k % 2

    def origin(c, k):
        if SPLIT == 2:
            return k * 8 + ((y + 1 + c // 2) % 4) * 2 + (core + c) % 2
        return (k // 2) * 8 + ((y + c) % 4) * 2 + k % 2

    mine = zl if SPLIT == 2 else zl * 2 + core

    barrier = pltpu.get_barrier_semaphore()

    def greet(j, carry):
        pl.semaphore_signal(
            barrier, inc=1, device_id=(dp, (me + j) % EXPERTS), device_id_type=MESH
        )
        return carry

    lax.fori_loop(1, EXPERTS, greet, 0)
    for i in range(1, NX):
        pl.semaphore_signal(barrier, inc=1, device_id=(x_peer(i), me), device_id_type=MESH)

    @pl.when(zh == 0)
    def greet_upper():
        pl.semaphore_signal(
            barrier, inc=1, device_id=(z_peer, me), device_id_type=MESH
        )


    load1.start()
    load2.start()
    loads[0].wait()
    loads[1].wait()

    ids = lax.broadcasted_iota(jnp.int32, (EXPERTS, toks), 0)
    member = jnp.zeros((EXPERTS, toks), F32)
    gates = jnp.zeros((EXPERTS, toks), F32)
    for k in range(routing_ref.shape[0]):
        hit = routing_ref[k : k + 1, :] == ids
        member = jnp.where(hit, 1.0, member)
        gates = jnp.where(hit, gate_ref[k : k + 1, :], gates)
    earlier = lax.broadcasted_iota(jnp.int32, (toks, toks), 0) < lax.broadcasted_iota(
        jnp.int32, (toks, toks), 1
    )
    earlier = jnp.where(earlier, 1.0, 0.0).astype(BF16)
    rank = jnp.dot(member.astype(BF16), earlier, preferred_element_type=F32)
    rank = jnp.where(member > 0.0, rank, -1.0).astype(BF16)
    slots = EXPERTS * SLOTS
    ids = lax.broadcasted_iota(jnp.int32, (1, EXPERTS), 1)
    place_of = (y + 3 - ((ids >> 1) & 3)) & 3
    if SPLIT == 2:
        place_of = (place_of * 2 + ((core + ids) & 1)) * PER + (ids >> 3)
    else:
        place_of = place_of * PER + (ids >> 3) * 2 + (ids & 1)
    spread = (
        lax.broadcasted_iota(jnp.int32, (slots, EXPERTS), 0) >> 4
    ) == place_of
    spread = jnp.where(spread, 1.0, 0.0).astype(BF16)
    within = lax.broadcasted_iota(jnp.int32, (slots, toks), 0) & (SLOTS - 1)
    hits = jnp.dot(spread, rank, preferred_element_type=F32) == within.astype(F32)
    high = gates.astype(BF16)
    low = (gates - high.astype(F32)).astype(BF16)
    place[...] = jnp.where(hits, 1.0, 0.0).astype(BF16)

    def gate_tables():
        whi[...] = jnp.where(
            hits, jnp.dot(spread, high, preferred_element_type=F32), 0.0
        ).astype(BF16)
        wlo[...] = jnp.where(
            hits, jnp.dot(spread, low, preferred_element_type=F32), 0.0
        ).astype(BF16)

    def pick_tokens(c):
        at = pl.ds(c * ROWS, ROWS)
        rows = jnp.dot(place[at, :], tok_ref[...], preferred_element_type=F32)
        send[c, :, 0] = rows.astype(BF16).reshape(PER, SLOTS, width)

    def pick_cotangents(c):
        at = pl.ds(c * ROWS, ROWS)
        rows = jnp.dot(whi[at, :], cot_ref[...], preferred_element_type=F32)
        rows += jnp.dot(wlo[at, :], cot_ref[...], preferred_element_type=F32)
        send[c, :, 1] = rows.astype(BF16).reshape(PER, SLOTS, width)

    def rows_part(ref, q, pieces):
        return ref if pieces == 1 else ref.at[q]

    def columns(q, pieces):
        return pl.ds(q * (3 * half // pieces), 3 * half // pieces)

    def dispatch_copy(c, j, q):
        k = (mine + j) % PER
        to = target(c, k)
        return pltpu.make_async_remote_copy(
            src_ref=rows_part(send.at[c, k], q, DP),
            dst_ref=rows_part(recv.at[c, mine], q, DP),
            send_sem=d_send.at[c, q, j],
            recv_sem=d_recv.at[c, q, mine],
            device_id=(dp, to),
            device_id_type=MESH,
        )

    def own_dispatch(q):
        return pltpu.make_async_copy(
            rows_part(send.at[OWN, mine], q, DP),
            rows_part(recv.at[OWN, mine], q, DP),
            d_recv.at[OWN, q, mine],
        )

    def return_copy(c, j, q):
        k = (mine + j) % PER
        to = origin(c, k)
        return pltpu.make_async_remote_copy(
            src_ref=rows_part(rsend.at[c, k], q, RP),
            dst_ref=rows_part(rrecv.at[c, mine], q, RP),
            send_sem=r_send.at[c, q, j],
            recv_sem=r_recv.at[c, q, mine],
            device_id=(dp, to),
            device_id_type=MESH,
        )

    def own_return(q):
        return pltpu.make_async_copy(
            rows_part(rsend.at[OWN, mine], q, RP),
            rows_part(rrecv.at[OWN, mine], q, RP),
            r_recv.at[OWN, q, mine],
        )

    def scatter_copy(c, i, q):
        to = (x + i) % NX
        return pltpu.make_async_remote_copy(
            src_ref=part.at[c, pl.ds(to * QUART, QUART), columns(q, XP)],
            dst_ref=xrecv.at[c, i - 1, :, columns(q, XP)],
            send_sem=x_send.at[c, i - 1, q],
            recv_sem=x_recv.at[c, i - 1, q],
            device_id=(x_peer(i), me),
            device_id_type=MESH,
        )

    def exchange_copy(c, q):
        return pltpu.make_async_remote_copy(
            src_ref=zsend.at[c, :, columns(q, ZP)],
            dst_ref=zrecv.at[c, :, columns(q, ZP)],
            send_sem=z_send.at[c, q],
            recv_sem=z_recv.at[c, q],
            device_id=(z_peer, me),
            device_id_type=MESH,
        )

    def gather_copy(c, i, owner, q):
        block = pl.ds(owner * QUART, QUART)
        return pltpu.make_async_remote_copy(
            src_ref=act.at[c, block, columns(q, AP)],
            dst_ref=act.at[c, block, columns(q, AP)],
            send_sem=g_send.at[c, i - 1, q],
            recv_sem=g_recv.at[c, i - 1, q],
            device_id=(x_peer(i), me),
            device_id_type=MESH,
        )

    def send_rows(c, q):
        if c == OWN:
            own_dispatch(q).start()

        def one(j, carry):
            dispatch_copy(c, j, q).start()
            return carry

        lax.fori_loop(1 if c == OWN else 0, PER, one, 0)

    def start_dispatch(c):
        if c > 0:
            pick_tokens(c)
        if DP == 2:
            send_rows(c, 0)
        if c == 0:
            gate_tables()
            loads[3].wait()
        pick_cotangents(c)
        send_rows(c, DP - 1)

    def wait_rows(c, q):
        def one(k, carry):
            block = rows_part(recv.at[c, k], q, DP)
            pltpu.make_async_copy(block, block, d_recv.at[c, q, k]).wait()
            return carry

        lax.fori_loop(0, PER, one, 0)

    def wait_dispatch(c):
        pass

    def products(c):
        if c == 0:
            load1.wait()
            load2.wait()
        wait_rows(c, 0)
        tile = 512

        def hidden_tile(n, carry):
            at = pl.ds(pl.multiple_of(n * tile, tile), tile)
            part[c, :, at] = jnp.dot(
                recv[c, :, 0].reshape(ROWS, width), w1[:, at], preferred_element_type=F32
            ).astype(BF16)
            return carry

        lax.fori_loop(0, 2 * half // tile, hidden_tile, 0)
        if XP == 3:
            for q in range(2):
                for i in range(1, NX):
                    scatter_copy(c, i, q).start()
        if DP == 2:
            wait_rows(c, 1)

        def act_tile(n, carry):
            at = pl.ds(pl.multiple_of(n * tile, tile), tile)
            to = pl.ds(pl.multiple_of(2 * half + n * tile, tile), tile)
            part[c, :, to] = lax.dot_general(
                recv[c, :, 1].reshape(ROWS, width), w2[at, :], LAST, preferred_element_type=F32
            ).astype(BF16)
            return carry

        lax.fori_loop(0, half // tile, act_tile, 0)
        for q in range(2 if XP == 3 else 0, XP):
            for i in range(1, NX):
                scatter_copy(c, i, q).start()

    def reduce_x(c):
        if c == 0:

            @pl.when(zh == 0)
            def upper_is_in():
                pl.semaphore_wait(ready, 1)

        for q in range(XP):
            for i in range(1, NX):
                scatter_copy(c, i, q).wait_recv()
        own = part[c, pl.ds(pl.multiple_of(x * QUART, QUART), QUART)].astype(F32)
        total = own + xrecv[c, 0].astype(F32)
        total += xrecv[c, 1].astype(F32)
        total += xrecv[c, 2].astype(F32)
        zsend[c] = total.astype(BF16)
        for q in range(ZP):
            exchange_copy(c, q).start()

    def activate(c):
        for q in range(ZP):
            exchange_copy(c, q).wait_recv()
        total = zsend[c].astype(F32) + zrecv[c].astype(F32)
        gate = total[:, :half]
        up = total[:, half : 2 * half]
        grad = total[:, 2 * half :]
        sig = jax.nn.sigmoid(gate)
        silu = gate * sig
        block = pl.ds(pl.multiple_of(x * QUART, QUART), QUART)
        act[c, block, 0:half] = (silu * up).astype(BF16)
        act[c, block, half : 2 * half] = (
            grad * up * sig * (1.0 + gate * (1.0 - sig))
        ).astype(BF16)
        act[c, block, 2 * half :] = (grad * silu).astype(BF16)
        for q in range(AP):
            for i in range(1, NX):
                gather_copy(c, i, x, q).start()

    def results(c):
        for q in range(AP):
            for i in range(1, NX):
                gather_copy(c, i, (x + NX - i) % NX, q).wait_recv()
        out = jnp.dot(act[c, :, 0:half], w2[...], preferred_element_type=F32)
        rsend[c, :, 0] = out.astype(BF16).reshape(PER, SLOTS, width)
        if RP == 2:
            send_results(c, 0)
        out = lax.dot_general(
            act[c, :, half:], w1[...], LAST, preferred_element_type=F32
        )
        rsend[c, :, 1] = out.astype(BF16).reshape(PER, SLOTS, width)
        send_results(c, RP - 1)

    def send_results(c, q):
        if c == OWN:
            own_return(q).start()

        def one(j, carry):
            return_copy(c, j, q).start()
            return carry

        lax.fori_loop(1 if c == OWN else 0, PER, one, 0)

    def transposes():
        place_t[...] = place[...].T
        whi_t[...] = whi[...].T
        wlo_t[...] = wlo[...].T

    def wait_results(c):
        def arrived(k, carry):
            for q in range(RP):
                block = rows_part(rrecv.at[c, k], q, RP)
                pltpu.make_async_copy(block, block, r_recv.at[c, q, k]).wait()
            return carry

        lax.fori_loop(0, PER, arrived, 0)

    def combine(c):
        wait_results(c)
        at = pl.ds(c * ROWS, ROWS)
        back = rrecv[c, :, 0].reshape(ROWS, width)
        mixed = jnp.dot(whi_t[:, at], back, preferred_element_type=F32)
        mixed += jnp.dot(wlo_t[:, at], back, preferred_element_type=F32)
        back = rrecv[c, :, 1].reshape(ROWS, width)
        grads = jnp.dot(place_t[:, at], back, preferred_element_type=F32)
        if c > 0:
            mixed += mixed_sum[...]
            grads += grad_sum[...]
        mixed_sum[...] = mixed
        grad_sum[...] = grads

    def hand_over(_):
        at = pl.ds((CHUNKS - 1) * ROWS, ROWS)
        for n, table in enumerate((whi_t, wlo_t, place_t)):
            last_tables[n] = table[:, at]

    def last_arrivals(_):
        wait_results(CHUNKS - 1)
        for q in range(2):
            last_rows[q] = rrecv[CHUNKS - 1, :, q].reshape(ROWS, width)

    loads[2].wait()
    pick_tokens(0)
    pl.semaphore_wait(barrier, EXPERTS - 1 + NX - 1 + zh)

    @pl.when(zh == 1)
    def answer():
        pl.semaphore_signal(ready, inc=1, device_id=(z_peer, me), device_id_type=MESH)


    run = {
        "D": start_dispatch,
        "d": wait_dispatch,
        "p": products,
        "r": reduce_x,
        "z": activate,
        "g": results,
    }
    def output_gradient(_):
        tile = 256

        def one(n, carry):
            at = pl.ds(pl.multiple_of(n * tile, tile), tile)
            ograd_ref[at, :] = lax.dot_general(
                act[:, :, at].reshape(slots, tile),
                recv[:, :, 1].reshape(slots, width),
                FIRST,
                preferred_element_type=F32,
            ).astype(BF16)
            return carry

        lax.fori_loop(0, half // tile, one, 0)

    def hidden_gradient(_):
        tile = 256
        rows_t[...] = recv[:, :, 0].reshape(slots, width).T

        def one(n, carry):
            at = pl.ds(pl.multiple_of(n * tile, tile), tile)
            cots = act[:, :, pl.ds(pl.multiple_of(half + n * tile, tile), tile)]
            hgrad_ref[:, at] = jnp.dot(
                rows_t[...], cots.reshape(slots, tile), preferred_element_type=F32
            ).astype(BF16)
            return carry

        lax.fori_loop(0, 2 * half // tile, one, 0)

    run["t"] = lambda _: transposes()
    run["o"] = output_gradient
    run["h"] = hidden_gradient
    run["c"] = combine
    run["l"] = hand_over
    run["a"] = last_arrivals
    for step in SCHEDULE:
        run[step[0]](int(step[1]))

    for c in range(CHUNKS):

        def left(j, carry):
            for q in range(DP):
                dispatch_copy(c, j, q).wait_send()
            for q in range(RP):
                return_copy(c, j, q).wait_send()
            return carry

        lax.fori_loop(1 if c == OWN else 0, PER, left, 0)
        for i in range(1, NX):
            for q in range(XP):
                scatter_copy(c, i, q).wait_send()
            for q in range(AP):
                gather_copy(c, i, x, q).wait_send()
        for q in range(ZP):
            exchange_copy(c, q).wait_send()


def store_kernel(
    mixed_sum,
    grad_sum,
    hgrad,
    ograd,
    rows,
    tables,
    mixed_out,
    tgrad_out,
    hgrad_out,
    ograd_out,
    mixed,
    tgrad,
    sem,
):
    pairs = ((hgrad, hgrad_out), (ograd, ograd_out), (mixed, mixed_out), (tgrad, tgrad_out))
    copies = [pltpu.make_async_copy(*pair, sem.at[i]) for i, pair in enumerate(pairs)]
    copies[0].start()
    copies[1].start()
    total = mixed_sum[...] + jnp.dot(tables[0], rows[0], preferred_element_type=F32)
    total += jnp.dot(tables[1], rows[0], preferred_element_type=F32)
    mixed[...] = total.astype(BF16)
    copies[2].start()
    total = grad_sum[...] + jnp.dot(tables[2], rows[1], preferred_element_type=F32)
    tgrad[...] = total.astype(BF16)
    copies[3].start()
    for copy in copies:
        copy.wait()


def body(tokens, cotangent, routing, gate_values, hidden_weight, output_weight):
    toks, width = tokens.shape
    half = output_weight.shape[1]
    wide = 3 * half
    dma = pltpu.SemaphoreType.DMA
    vmem = pl.BlockSpec(memory_space=pltpu.VMEM)
    hbm = pl.BlockSpec(memory_space=pltpu.HBM)
    shapes = ((toks, width), (toks, width), (width, 2 * half), (half, width))
    slots = EXPERTS * SLOTS
    made = pl.pallas_call(
        kernel,
        name="moe_layer",
        out_shape=[pltpu.VMEM(shape, F32) for shape in shapes[:2]]
        + [pltpu.VMEM(shape, BF16) for shape in shapes[2:]]
        + [pltpu.VMEM((2, ROWS, width), BF16), pltpu.VMEM((3, toks, ROWS), BF16)],
        in_specs=[hbm] * 6,
        out_specs=[vmem] * 6,
        scratch_shapes=[
            pltpu.VMEM(routing.shape[::-1], jnp.int32),
            pltpu.VMEM(routing.shape[::-1], F32),
            pltpu.VMEM((toks, width), BF16),
            pltpu.VMEM((toks, width), BF16),
            pltpu.VMEM((width, 2 * half), BF16),
            pltpu.VMEM((half, width), BF16),
            pltpu.VMEM((slots, toks), BF16),
            pltpu.VMEM((slots, toks), BF16),
            pltpu.VMEM((slots, toks), BF16),
            pltpu.VMEM((CHUNKS, PER, 2, SLOTS, width), BF16),
            pltpu.VMEM((CHUNKS, PER, 2, SLOTS, width), BF16),
            pltpu.VMEM((CHUNKS, ROWS, wide), BF16),
            pltpu.VMEM((CHUNKS, NX - 1, QUART, wide), BF16),
            pltpu.VMEM((CHUNKS, QUART, wide), BF16),
            pltpu.VMEM((CHUNKS, QUART, wide), BF16),
            pltpu.VMEM((CHUNKS, ROWS, wide), BF16),
            pltpu.VMEM((CHUNKS, PER, 2, SLOTS, width), BF16),
            pltpu.VMEM((CHUNKS, PER, 2, SLOTS, width), BF16),
            pltpu.VMEM((width, slots), BF16),
            pltpu.VMEM((toks, slots), BF16),
            pltpu.VMEM((toks, slots), BF16),
            pltpu.VMEM((toks, slots), BF16),
            pltpu.SemaphoreType.REGULAR,
            dma((6,)),
            dma((CHUNKS, DP, PER)),
            dma((CHUNKS, DP, PER)),
            dma((CHUNKS, NX - 1, XP)),
            dma((CHUNKS, NX - 1, XP)),
            dma((CHUNKS, ZP)),
            dma((CHUNKS, ZP)),
            dma((CHUNKS, NX - 1, AP)),
            dma((CHUNKS, NX - 1, AP)),
            dma((CHUNKS, RP, PER)),
            dma((CHUNKS, RP, PER)),
        ],
        compiler_params=pltpu.CompilerParams(
            collective_id=0, has_side_effects=True, vmem_limit_bytes=VMEM_LIMIT
        ),
    )(
        *[
            pltpu.with_memory_space_constraint(value, pltpu.HBM)
            for value in (
                routing.T,
                gate_values.T,
                tokens,
                cotangent,
                hidden_weight[0],
                output_weight[0],
            )
        ]
    )
    made = [pltpu.with_memory_space_constraint(value, pltpu.VMEM) for value in made]
    mixed, token_grad, hidden_grad, output_grad = pl.pallas_call(
        store_kernel,
        name="store",
        out_shape=[jax.ShapeDtypeStruct(shape, BF16) for shape in shapes],
        in_specs=[vmem] * 6,
        out_specs=[hbm] * 4,
        scratch_shapes=[
            pltpu.VMEM((toks, width), BF16),
            pltpu.VMEM((toks, width), BF16),
            dma((4,)),
        ],
        compiler_params=pltpu.CompilerParams(vmem_limit_bytes=8 * 2**20),
    )(*made)
    return mixed, token_grad, hidden_grad[None], output_grad[None]


def solution(mesh):
    return jax.shard_map(
        body,
        mesh=mesh,
        in_specs=(
            P("expert", "dp"),
            P("expert", "dp"),
            P("expert", None),
            P("expert", None),
            P("expert", "dp", None),
            P("expert", None, "dp"),
        ),
        out_specs=(
            P("expert", "dp"),
            P("expert", "dp"),
            P("expert", "dp", None),
            P("expert", None, "dp"),
        ),
        check_vma=False,
    )
```
